256 devices in a mesh: frame: 8 (over z), tile: 32 (over x, y, core).
Axes of the slice: x: 4, y: 4, z: 8, core: 2. Of those that a mesh axis runs over, the one named last changes fastest.
Arguments:
- displacement: bfloat16 [512, 2, 32, 4096], P('frame', None, 'tile'), may hold values from -256 to 256
Outputs:
- basis: bfloat16 [512, 3, 32, 4096], P(None, None, 'tile', 'frame')
- factor: float32 [512, 512], replicated
The draws below stay inside these ranges and needn't reach their ends.
All inputs are finite; a program needn't handle non-finite values.
Results may differ from the reference program's by a relative error of at most 0.0053.
The reference program's roundings to bfloat16 on the way (of `strain`) count: a program that leaves them out, or rounds other values in their place, can miss the bound.
Values may be sent and summed in bfloat16 or wider, within the bound.
No kernel may reach another device: no remote copies, remote signals or barrier semaphores. Data moves between devices by JAX's collectives and lax.ppermute only.
A program may use at most 64 MiB of HBM per device.

```python
import math
import jax
import jax.numpy as jnp
from jax import lax

F = 512
W = 4096
H = 32


def draw_displacement(key, part):
    keys = jax.random.split(jax.random.fold_in(key, 11), 4)
    noise = jax.random.truncated_normal(keys[0], -4.0, 4.0, (F, 2, H, W), jnp.float32)
    scales = jnp.exp(jax.random.uniform(keys[1], (F,), jnp.float32, math.log(0.5), math.log(2.0)))
    weight = 0.3
    modes = jax.random.truncated_normal(keys[2], -4.0, 4.0, (4, 2, H, W), jnp.float32)
    coeffs = jax.random.truncated_normal(keys[3], -3.0, 3.0, (F, 4), jnp.float32)
    field = noise
    for index in range(4):
        field = field + weight * coeffs[:, index][:, None, None, None] * modes[index][None]
    ramp_rows = 1.0 + (math.sqrt(3.0) - 1.0) * jnp.arange(H, dtype=jnp.float32) / max(H - 1, 1)
    ramp_cols = 1.0 + (math.sqrt(3.0) - 1.0) * jnp.arange(W, dtype=jnp.float32) / max(W - 1, 1)
    return (scales[:, None, None, None] * field * ramp_rows[None, None, :, None] * ramp_cols[None, None, None, :]).astype(jnp.bfloat16)


def setup_inputs(seed: int = 0) -> dict:
    seeds = jax.random.split(jax.random.key(seed), 2)
    return {
        "displacement": draw_displacement(jax.random.fold_in(seeds[1], 71), 0),
    }


def derivative(center, before, after, first, final):
    return jnp.where(first, after - center, jnp.where(final, center - before, (after - before) * 0.5))

def column_derivative(center):
    width = center.shape[-1]
    after = jnp.concatenate([center[..., 1:], center[..., -1:]], axis=-1)
    before = jnp.concatenate([center[..., :1], center[..., :-1]], axis=-1)
    column = jnp.arange(width, dtype=jnp.int32)
    return derivative(center, before, after, column == 0, column == width - 1)

def strain_row(displacement, row):
    height = displacement.shape[2]
    above_row = jnp.maximum(row - 1, 0).astype(jnp.int32)
    below_row = jnp.minimum(row + 1, height - 1).astype(jnp.int32)
    center = lax.dynamic_index_in_dim(displacement, row, 2, keepdims=False).astype(jnp.float32)
    above = lax.dynamic_index_in_dim(displacement, above_row, 2, keepdims=False).astype(jnp.float32)
    below = lax.dynamic_index_in_dim(displacement, below_row, 2, keepdims=False).astype(jnp.float32)
    d_rows = derivative(center, above, below, row == 0, row == height - 1)
    d_cols = column_derivative(center)
    strain = jnp.stack([d_cols[:, 0], d_rows[:, 1], 0.5 * (d_rows[:, 0] + d_cols[:, 1])], axis=1)
    return strain.astype(jnp.bfloat16)

def reference(displacement):
    frames = displacement.shape[0]
    height = displacement.shape[2]
    width = displacement.shape[3]
    scale = math.sqrt(3 * height * width)

    def accumulate(gram, row):
        strain = strain_row(displacement, row)
        flat = strain.reshape(frames, 3 * width)
        gram = gram + lax.dot_general(flat.astype(jnp.float32), flat.astype(jnp.float32), (((1,), (1,)), ((), ())), preferred_element_type=jnp.float32)
        return (gram, strain)
    gram, strains = lax.scan(accumulate, jnp.zeros((frames, frames), jnp.float32), jnp.arange(height, dtype=jnp.int32))
    lower = jnp.linalg.cholesky(gram)

    def solve(strain):
        flat = strain.reshape(frames, 3 * width).astype(jnp.float32)
        solved = lax.linalg.triangular_solve(lower, flat, left_side=True, lower=True)
        return (solved * scale).astype(jnp.bfloat16)
    basis_rows = lax.map(solve, strains)
    basis = jnp.transpose(basis_rows.reshape(height, frames, 3, width), (1, 2, 0, 3))
    return (basis, lower.T / scale)
```

```python
import math

import jax
import jax.numpy as jnp
from jax import lax
from jax.sharding import Mesh, PartitionSpec as P

TILE = ("x", "y", "core")


def with_halo(array, sides, width):
    for axis, dim in sides:
        peers, length = (lax.axis_size(axis), array.shape[dim])
        up = [(i, (i + 1) % peers) for i in range(peers - 1)]
        down = [(j, i) for i, j in up]
        last = lax.slice_in_dim(array, length - width, length, axis=dim)
        first = lax.slice_in_dim(array, 0, width, axis=dim)
        before = lax.ppermute(last, axis, up)
        after = lax.ppermute(first, axis, down)
        array = jnp.concatenate([before, array, after], axis=dim)
    return array


def derivative(center, before, after, first, final):
    return jnp.where(
        first, after - center, jnp.where(final, center - before, (after - before) * 0.5)
    )


def column_derivative(center):
    width = center.shape[-1]
    after = jnp.concatenate([center[..., 1:], center[..., -1:]], axis=-1)
    before = jnp.concatenate([center[..., :1], center[..., :-1]], axis=-1)
    column = jnp.arange(width, dtype=jnp.int32)
    return derivative(center, before, after, column == 0, column == width - 1)


def combine_strain(d_rows, d_cols):
    return jnp.stack(
        [d_cols[:, 0], d_rows[:, 1], 0.5 * (d_rows[:, 0] + d_cols[:, 1])], axis=1
    ).astype(jnp.bfloat16)


def other_core_half(array, mine):
    half = array.shape[0] // 2
    return lax.dynamic_slice_in_dim(array, (1 - mine) * half, half, 0)


def sum_devices(array):
    rows, width = array.shape
    swap = [(0, 1), (1, 0)]
    core = lax.axis_index("core")
    half = rows // 2
    kept = lax.dynamic_slice_in_dim(array, core * half, half, 0)
    kept = kept + lax.ppermute(other_core_half(array, core), "core", swap)
    plane = lax.axis_size("x") * lax.axis_size("y")
    part = half // plane
    pieces = lax.all_to_all(kept.reshape(plane, part, width), ("x", "y"), 0, 0, tiled=True)
    piece = pieces.sum(0)
    depth = lax.axis_size("z")
    copies = jnp.broadcast_to(piece[None], (depth, part, width))
    piece = lax.all_to_all(copies, "z", 0, 0, tiled=True).sum(0)
    copies = jnp.broadcast_to(piece[None], (plane, part, width))
    kept = lax.all_to_all(copies, ("x", "y"), 0, 0, tiled=True).reshape(half, width)
    other = lax.ppermute(kept, "core", swap)
    first = jnp.where(core == 0, kept, other)
    second = jnp.where(core == 0, other, kept)
    return jnp.concatenate([first, second], 0)


def local(displacement):
    rows = displacement.shape[2]
    full_width = displacement.shape[3]
    total_rows = lax.axis_size(TILE) * rows
    scale = math.sqrt(3 * total_rows * full_width)
    row_global = lax.axis_index(TILE) * rows + jnp.arange(rows, dtype=jnp.int32)
    first = (row_global == 0)[:, None]
    final = (row_global == total_rows - 1)[:, None]
    padded = with_halo(displacement, ((TILE, 2),), 1)
    field = padded.astype(jnp.float32)
    center = field[:, :, 1:-1, :]
    d_rows = derivative(center, field[:, :, :-2, :], field[:, :, 2:, :], first, final)
    d_cols = column_derivative(center)
    strain = combine_strain(d_rows, d_cols)
    pixel_major = lax.all_to_all(strain, "z", split_axis=3, concat_axis=0, tiled=True)
    frames = pixel_major.shape[0]
    snapshot_half = pixel_major.reshape(frames, -1)
    local_gram = lax.dot_general(
        snapshot_half, snapshot_half, (((1,), (1,)), ((), ())), preferred_element_type=jnp.float32
    )
    gram = sum_devices(local_gram)
    lower = jnp.linalg.cholesky(gram)
    snapshot = snapshot_half.astype(jnp.float32)
    solved = lax.linalg.triangular_solve(lower, snapshot, left_side=True, lower=True)
    basis = (solved * scale).astype(jnp.bfloat16).reshape(pixel_major.shape)
    return (basis, lower.T / scale)


def solution(mesh):
    frames, tiles = mesh.devices.shape
    side = math.isqrt(tiles // 2)
    split = Mesh(mesh.devices.reshape(frames, side, side, 2), ("z",) + TILE)
    return jax.shard_map(
        local,
        mesh=split,
        in_specs=(P("z", None, TILE, None),),
        out_specs=(P(None, None, TILE, "z"), P()),
        check_vma=False,
    )
```

```python
import functools
import math

import jax
import jax.numpy as jnp
from jax import lax
from jax.experimental import pallas as pl
from jax.experimental.pallas import tpu as pltpu
from jax.sharding import Mesh, PartitionSpec as P

TILE = ("x", "y", "core")
SUB = 8
BLOCK = 128
HIGH = lax.Precision.HIGHEST
F32 = jnp.float32
BF16 = jnp.bfloat16
VMEM = pl.BlockSpec(memory_space=pltpu.VMEM)
SMEM = pl.BlockSpec(memory_space=pltpu.SMEM)
PARAMS = pltpu.CompilerParams(vmem_limit_bytes=40 << 20)


def column_derivative(center):
    width = center.shape[-1]
    column = lax.broadcasted_iota(jnp.int32, center.shape, center.ndim - 1)
    first, final = column == 0, column == width - 1
    after = jnp.where(final, center, pltpu.roll(center, width - 1, center.ndim - 1))
    before = jnp.where(first, center, pltpu.roll(center, 1, center.ndim - 1))
    return (after - before) * jnp.where(first | final, 1.0, 0.5)


def row_derivative(center, before, after, first, final):
    after = jnp.where(final, center, after)
    before = jnp.where(first, center, before)
    return (after - before) * jnp.where(first | final, 1.0, 0.5)


def scatter_columns(whole_ref, place, outs):
    peers = len(outs)
    width = outs[0].shape[-1]
    for shift in range(peers):
        start = pl.multiple_of(lax.rem(place + shift, peers) * width, width)
        outs[shift][...] = whole_ref[..., pl.ds(start, width)]


def normal_kernel(where_ref, center_ref, *refs):
    outs, whole_ref = refs[:-1], refs[-1]
    whole_ref[...] = column_derivative(center_ref[0].astype(F32)).astype(BF16)
    scatter_columns(whole_ref, where_ref[0], outs)


def shear_kernel(where_ref, center_ref, before_ref, after_ref, *refs):
    outs, whole_ref = refs[:-1], refs[-1]
    first, final = where_ref[1] == 0, where_ref[1] == where_ref[2] - 1
    u, v = center_ref[0].astype(F32), center_ref[1].astype(F32)
    u_rows = row_derivative(u, before_ref[0].astype(F32), after_ref[0].astype(F32), first, final)
    v_rows = row_derivative(v, before_ref[1].astype(F32), after_ref[1].astype(F32), first, final)
    whole_ref[0] = v_rows.astype(BF16)
    whole_ref[1] = (0.5 * (u_rows + column_derivative(v))).astype(BF16)
    scatter_columns(whole_ref, where_ref[0], outs)


def strain_blocks(kernel, where, arrays, peers, out_block):
    width = arrays[0].shape[-1]
    block = jax.ShapeDtypeStruct(out_block + (width // peers,), BF16)
    return pl.pallas_call(
        kernel,
        in_specs=[SMEM] + [VMEM] * len(arrays),
        out_specs=[VMEM] * peers,
        out_shape=[block] * peers,
        scratch_shapes=[pltpu.VMEM(out_block + (width,), BF16)],
        compiler_params=PARAMS,
        name=kernel.__name__,
    )(where, *arrays)


def upper_blocks(count):
    return [(i, j) for i in range(count) for j in range(i, count)]


def gram_kernel(where_ref, *refs, peers):
    normal, shear = refs[:peers], refs[peers:2 * peers]
    snap_ref, kept_ref, sent_ref, both_ref = refs[2 * peers:]
    frames = normal[0].shape[0]
    for shift in range(peers):
        source = lax.rem(where_ref[0] + peers - shift, peers)
        rows = pl.ds(pl.multiple_of(source * frames, frames), frames)
        snap_ref[0, rows, :] = normal[shift][...]
        snap_ref[1, rows, :] = shear[shift][0]
        snap_ref[2, rows, :] = shear[shift][1]
    pairs = upper_blocks(snap_ref.shape[1] // BLOCK)
    half = len(pairs) // 2
    for i in range(snap_ref.shape[1] // BLOCK):
        total = None
        for c in range(3):
            left = snap_ref[c, i * BLOCK:(i + 1) * BLOCK, :]
            right = snap_ref[c, i * BLOCK:, :]
            part = lax.dot_general(left, right, (((1,), (1,)), ((), ())), preferred_element_type=F32)
            total = part if total is None else total + part
        for n, (row, col) in enumerate(pairs):
            if row == i:
                both_ref[n // half, n % half] = total[:, (col - i) * BLOCK:(col - i + 1) * BLOCK]
    core = where_ref[3]
    kept_ref[...] = both_ref[core]
    sent_ref[...] = both_ref[1 - core]


def cross_products(where, normal, shear):
    peers = len(normal)
    frames, width = normal[0].shape
    count = frames * peers // BLOCK
    half = count * (count + 1) // 4
    part = jax.ShapeDtypeStruct((half, BLOCK, BLOCK), F32)
    return pl.pallas_call(
        functools.partial(gram_kernel, peers=peers),
        in_specs=[SMEM] + [VMEM] * (2 * peers),
        out_specs=[VMEM] * 3,
        out_shape=[jax.ShapeDtypeStruct((3, frames * peers, width), BF16), part, part],
        scratch_shapes=[pltpu.VMEM((2, half, BLOCK, BLOCK), F32)],
        compiler_params=PARAMS,
        name="gram_kernel",
    )(where, *normal, *shear)


def eliminate_block(rows):
    tiles = len(rows)
    lane = lax.broadcasted_iota(jnp.int32, (SUB, BLOCK), 1)
    sub = lax.broadcasted_iota(jnp.int32, (SUB, BLOCK), 0)
    upper, inverse = [], []
    rows = list(rows)
    for step in range(tiles):
        base = step * SUB
        block = rows[step]
        a = {}
        for j in range(SUB):
            column = jnp.broadcast_to(block[:, base + j:base + j + 1], (SUB, BLOCK))
            for i in range(j, SUB):
                a[i, j] = jnp.broadcast_to(column[i:i + 1, :], (SUB, BLOCK))
        inside = (lane >= base) & (lane < base + SUB)
        seeded = jnp.where(inside, (lane - base == sub).astype(F32), block)
        v = [jnp.broadcast_to(seeded[i:i + 1, :], (SUB, BLOCK)) for i in range(SUB)]
        unit = {}
        pivot, root = [], []
        for j in range(SUB):
            inv = 1.0 / a[j, j]
            pivot.append(inv)
            root.append(lax.rsqrt(a[j, j]))
            for i in range(j + 1, SUB):
                unit[i, j] = a[i, j] * inv
            for m in range(j + 1, SUB):
                for i in range(m, SUB):
                    a[i, m] = a[i, m] - (a[i, j] * a[m, j]) * inv
            for i in range(j + 1, SUB):
                v[i] = v[i] - unit[i, j] * v[j]
        z = [v[j] * pivot[j] for j in range(SUB)]
        done = jnp.zeros((SUB, BLOCK), F32)
        corner = jnp.zeros((SUB, BLOCK), F32)
        for i in range(SUB):
            line = jnp.zeros((SUB, BLOCK), F32)
            for m in range(i, SUB):
                line = jnp.where(lane == base + m, a[m, i], line)
            done = jnp.where(sub == i, v[i] * root[i], done)
            corner = jnp.where(sub == i, line * root[i], corner)
        upper.append(jnp.where(lane >= base + SUB, done, corner))
        inverse.append(jnp.where(lane < base + SUB, done, 0.0))
        for q in range(step + 1, tiles):
            old = rows[q]
            acc = jnp.where(inside, 0.0, old)
            left = [jnp.broadcast_to(old[:, base + j:base + j + 1], (SUB, BLOCK)) for j in range(SUB)]
            for j in range(SUB):
                for m in range(j + 1, SUB):
                    left[m] = left[m] - left[j] * unit[m, j]
                acc = acc - left[j] * z[j]
            rows[q] = acc
    return upper, inverse


def span(k):
    return slice(k * BLOCK, (k + 1) * BLOCK)


def factor_kernel(where_ref, kept_ref, other_ref, factor_ref, hi_ref, lo_ref, both_ref, m_ref, t_ref, *, scale):
    n = m_ref.shape[0]
    blocks = n // BLOCK
    core = where_ref[3]
    both_ref[core] = kept_ref[...]
    both_ref[1 - core] = other_ref[...]
    pairs = upper_blocks(blocks)
    half = len(pairs) // 2
    for k in range(1, blocks):
        m_ref[span(k), :k * BLOCK] = jnp.zeros((BLOCK, k * BLOCK), F32)
    for index, (row, col) in enumerate(pairs):
        m_ref[span(row), span(col)] = both_ref[index // half, index % half]
    for k in range(blocks):
        rows = [m_ref[k * BLOCK + s:k * BLOCK + s + SUB, span(k)] for s in range(0, BLOCK, SUB)]
        upper, inverse = eliminate_block(rows)
        for s in range(BLOCK // SUB):
            t_ref[s * SUB:(s + 1) * SUB, :] = inverse[s]
            factor_ref[k * BLOCK + s * SUB:k * BLOCK + (s + 1) * SUB, span(k)] = upper[s] * (1.0 / scale)
        t = t_ref[...]
        m_ref[span(k), :] = lax.dot_general(t, m_ref[span(k), :], (((1,), (0,)), ((), ())), precision=HIGH, preferred_element_type=F32)
        m_ref[span(k), span(k)] = t
        rest = n - (k + 1) * BLOCK
        if rest:
            panel = m_ref[span(k), :]
            below = slice((k + 1) * BLOCK, n)
            m_ref[below, span(k)] = jnp.zeros((rest, BLOCK), F32)
            m_ref[below, :] = m_ref[below, :] - lax.dot_general(panel[:, (k + 1) * BLOCK:], panel, (((0,), (0,)), ((), ())), precision=HIGH, preferred_element_type=F32)
    col = lax.broadcasted_iota(jnp.int32, (BLOCK, n), 1)
    for k in range(blocks):
        whole = m_ref[span(k), :]
        if k + 1 < blocks:
            factor_ref[span(k), (k + 1) * BLOCK:] = whole[:, (k + 1) * BLOCK:] * (1.0 / scale)
        if k:
            factor_ref[span(k), :k * BLOCK] = jnp.zeros((BLOCK, k * BLOCK), F32)
        inv = jnp.where(col < (k + 1) * BLOCK, whole, 0.0) * scale
        hi = inv.astype(BF16)
        hi_ref[span(k), :] = hi
        lo_ref[span(k), :] = (inv - hi.astype(F32)).astype(BF16)


def factorize(where, kept, other, n, scale):
    return pl.pallas_call(
        functools.partial(factor_kernel, scale=scale),
        in_specs=[SMEM, VMEM, VMEM],
        out_specs=[VMEM] * 3,
        out_shape=[jax.ShapeDtypeStruct((n, n), F32)] + [jax.ShapeDtypeStruct((n, n), BF16)] * 2,
        scratch_shapes=[pltpu.VMEM((2,) + kept.shape, F32), pltpu.VMEM((n, n), F32), pltpu.VMEM((BLOCK, BLOCK), F32)],
        compiler_params=PARAMS,
        name="factor_kernel",
    )(where, kept, other)


def basis_kernel(hi_ref, lo_ref, snap_ref, out_ref):
    n = hi_ref.shape[0]
    chunk = n // 2
    for r in range(2):
        rows, depth = slice(r * chunk, (r + 1) * chunk), (r + 1) * chunk
        part = snap_ref[0, :depth, :]
        total = jnp.dot(hi_ref[rows, :depth], part, preferred_element_type=F32)
        total = total + jnp.dot(lo_ref[rows, :depth], part, preferred_element_type=F32)
        out_ref[0, rows, :] = total.astype(BF16)


def make_basis(hi, lo, snap):
    block = pl.BlockSpec((1,) + snap.shape[1:], lambda c: (c, 0, 0))
    return pl.pallas_call(
        basis_kernel,
        grid=(snap.shape[0],),
        in_specs=[VMEM, VMEM, block],
        out_specs=block,
        out_shape=jax.ShapeDtypeStruct(snap.shape, BF16),
        compiler_params=PARAMS,
        name="basis_kernel",
    )(hi, lo, snap)


def exchange(blocks, axis):
    peers = len(blocks)
    received = [blocks[0]]
    for shift in range(1, peers):
        received.append(lax.ppermute(blocks[shift], axis, [(i, (i + shift) % peers) for i in range(peers)]))
    return received


def sum_devices(kept, sent):
    swap = [(0, 1), (1, 0)]
    shape = kept.shape
    kept = (kept + lax.ppermute(sent, "core", swap)).reshape(-1, shape[-1])
    plane = lax.axis_size(("x", "y"))
    part, width = kept.shape[0] // plane, kept.shape[1]
    piece = lax.all_to_all(kept.reshape(plane, part, width), ("x", "y"), 0, 0, tiled=True).sum(0)
    copies = jnp.broadcast_to(piece[None], (lax.axis_size("z"), part, width))
    piece = lax.all_to_all(copies, "z", 0, 0, tiled=True).sum(0)
    copies = jnp.broadcast_to(piece[None], (plane, part, width))
    kept = lax.all_to_all(copies, ("x", "y"), 0, 0, tiled=True).reshape(shape)
    return kept, lax.ppermute(kept, "core", swap)


def local(displacement):
    frames, _, _, width = displacement.shape
    peers = lax.axis_size("z")
    total_rows = lax.axis_size(TILE)
    total_frames = frames * peers
    scale = math.sqrt(3 * total_rows * width)
    where = jnp.stack([lax.axis_index("z"), lax.axis_index(TILE), jnp.int32(total_rows), lax.axis_index("core")]).astype(jnp.int32)
    planes = displacement.reshape(frames, 2, width).transpose(1, 0, 2)
    up = [(i, i + 1) for i in range(total_rows - 1)]
    before = lax.ppermute(planes, TILE, up)
    after = lax.ppermute(planes, TILE, [(j, i) for i, j in up])
    normal = exchange(strain_blocks(normal_kernel, where, [planes], peers, (frames,)), "z")
    shear = exchange(strain_blocks(shear_kernel, where, [planes, before, after], peers, (2, frames)), "z")
    snap, kept, sent = cross_products(where, normal, shear)
    kept, other = sum_devices(kept, sent)
    factor, hi, lo = factorize(where, kept, other, total_frames, scale)
    basis = make_basis(hi, lo, snap)
    return basis.transpose(1, 0, 2)[:, :, None, :], factor


def solution(mesh):
    frames, tiles = mesh.devices.shape
    side = math.isqrt(tiles // 2)
    split = Mesh(mesh.devices.reshape(frames, side, side, 2), ("z",) + TILE)
    return jax.shard_map(
        local,
        mesh=split,
        in_specs=(P("z", None, TILE, None),),
        out_specs=(P(None, None, TILE, "z"), P()),
        check_vma=False,
    )
```

```python
import functools
import math

import jax
import jax.numpy as jnp
from jax import lax
from jax.experimental import pallas as pl
from jax.experimental.pallas import tpu as pltpu
from jax.sharding import Mesh, PartitionSpec as P

TILE = ("x", "y", "core")
SUB = 8
BLOCK = 128
LANES = 128
HIGH = lax.Precision.HIGHEST
F32 = jnp.float32
BF16 = jnp.bfloat16
VMEM = pl.BlockSpec(memory_space=pltpu.VMEM)
SMEM = pl.BlockSpec(memory_space=pltpu.SMEM)
PARAMS = pltpu.CompilerParams(vmem_limit_bytes=24 << 20)


def turns(sign):
    return [0, 2 * sign, -3, 3, -2 * sign, 4, -1, 1]


def spread_kernel(where_ref, planes_ref, *outs):
    place, core = where_ref[0], where_ref[3]
    own_ref, pair_ref = outs[0], outs[1]
    singles = dict(zip((2, 3, 4, 6, 7), outs[2:]))
    width = own_ref.shape[1]
    fields, frames, total = planes_ref.shape
    peers = total // width
    rows = fields * frames
    row = lax.broadcasted_iota(jnp.int32, (SUB, LANES), 0)
    lane = lax.broadcasted_iota(jnp.int32, (SUB, LANES), 1)
    last = ((row == 0) & (lane == LANES - 1)).astype(BF16)
    first = ((row == 1) & (lane == 0)).astype(BF16)
    for slot, offset in enumerate(turns(1 - 2 * core)):
        out_ref = own_ref if slot == 0 else pair_ref.at[0] if slot == 1 else pair_ref.at[1] if slot == 5 else singles[slot]
        start = lax.rem(place + offset + peers, peers) * width
        left = pl.multiple_of(jnp.maximum(start - LANES, 0), LANES)
        right = pl.multiple_of(jnp.minimum(start + width, total - LANES), LANES)
        out_ref[rows:, :] = jnp.zeros((SUB, width), BF16)
        for field in range(fields):
            part = slice(field * frames, (field + 1) * frames)
            out_ref[part, :] = planes_ref[field, :, pl.ds(pl.multiple_of(start, width), width)]
        below = planes_ref[:, :, pl.ds(left, LANES)].reshape(rows, LANES)
        above = planes_ref[:, :, pl.ds(right, LANES)].reshape(rows, LANES)
        dims = (((1,), (1,)), ((), ()))
        edges = lax.dot_general(last, below, dims, preferred_element_type=F32)
        edges = edges + lax.dot_general(first, above, dims, preferred_element_type=F32)
        out_ref[rows:, :rows] = edges.astype(BF16)


def spread(where, planes, peers):
    fields, frames, width = planes.shape
    block = jax.ShapeDtypeStruct((fields * frames + SUB, width // peers), BF16)
    pair = jax.ShapeDtypeStruct((2,) + block.shape, BF16)
    return pl.pallas_call(
        spread_kernel,
        in_specs=[SMEM, VMEM],
        out_specs=[VMEM] * 7,
        out_shape=[block, pair] + [block] * 5,
        compiler_params=PARAMS,
        name="spread_kernel",
    )(where, planes)


def collect_kernel(*refs):
    blocks, out_ref = refs[:-1], refs[-1]
    slot = 0
    for block in blocks:
        if len(block.shape) == 3:
            out_ref[slot] = block[0]
        else:
            out_ref[slot] = block[...]
        slot += 1


def collect(*blocks):
    return pl.pallas_call(
        collect_kernel,
        in_specs=[VMEM] * len(blocks),
        out_specs=VMEM,
        out_shape=jax.ShapeDtypeStruct((len(blocks),) + blocks[0].shape, BF16),
        compiler_params=PARAMS,
        name="collect_kernel",
    )(*blocks)


def shifted(block, near, far, peers):
    pairs = []
    for i in range(peers):
        pairs += [(2 * i, 2 * ((i + near) % peers)), (2 * i + 1, 2 * ((i + far) % peers) + 1)]
    return lax.ppermute(block, ("z", "core"), pairs)


def exchange(where, planes, peers):
    own, pair, minus3, plus3, back2, minus1, plus1 = spread(where, planes, peers)
    pair = shifted(pair, 2, -2, peers)
    minus3 = shifted(minus3, -3, -3, peers)
    plus3 = shifted(plus3, 3, 3, peers)
    first = collect(own, pair, minus3, plus3)
    back2 = shifted(back2, -2, 2, peers)
    relayed = shifted(pair[1], 2, -2, peers)
    minus1 = shifted(minus1, -1, -1, peers)
    plus1 = shifted(plus1, 1, 1, peers)
    second = collect(back2, relayed, minus1, plus1)
    return first, second


NEXT = (0, 4, 2, 3, 1, 5, 6, 7)


def row_derivative(center, before, after, first, final):
    after = jnp.where(final, center, after)
    before = jnp.where(first, center, before)
    return (after - before) * jnp.where(first | final, 1.0, 0.5)


def column_derivative(center, left, right, start, total):
    width = center.shape[1]
    lane = lax.broadcasted_iota(jnp.int32, center.shape, 1)
    column = lane + start
    first, final = column == 0, column == total - 1
    before = jnp.where(lane == 0, left, pltpu.roll(center, 1, 1))
    after = jnp.where(lane == width - 1, right, pltpu.roll(center, width - 1, 1))
    after = jnp.where(final, center, after)
    before = jnp.where(first, center, before)
    return (after - before) * jnp.where(first | final, 1.0, 0.5)


def upper_blocks(count):
    return [(i, j) for i in range(count) for j in range(i, count)]


def gram_kernel(where_ref, *refs):
    parts, snap_ref, kept_ref, sent_ref, both_ref = refs[:6], *refs[6:]
    center, before, after = parts[0:2], parts[2:4], parts[4:6]
    half_peers, _, width = center[0].shape
    peers = 2 * half_peers
    total = snap_ref.shape[1]
    frames = total // peers
    rows = 2 * frames
    top, bottom = where_ref[1] == 0, where_ref[1] == where_ref[2] - 1
    start = where_ref[0] * width
    row = lax.broadcasted_iota(jnp.int32, (SUB, LANES), 0)
    turn = (((0,), (0,)), ((), ()))
    for slot, offset in enumerate(turns(1 - 2 * where_ref[3])):
        here = center[slot // half_peers].at[slot % half_peers]
        beside = NEXT[slot]
        above = before[beside // half_peers].at[beside % half_peers]
        below = after[beside // half_peers].at[beside % half_peers]
        edges = here[rows:, :rows]
        left = lax.dot_general(edges, (row == 0).astype(BF16), turn, preferred_element_type=F32)
        right = lax.dot_general(edges, (row == 1).astype(BF16), turn, preferred_element_type=F32)
        u_rows, v_rows = slice(0, frames), slice(frames, rows)
        u, v = here[u_rows, :].astype(F32), here[v_rows, :].astype(F32)
        slope_u = row_derivative(u, above[u_rows, :].astype(F32), below[u_rows, :].astype(F32), top, bottom)
        slope_v = row_derivative(v, above[v_rows, :].astype(F32), below[v_rows, :].astype(F32), top, bottom)
        along_u = column_derivative(u, left[u_rows, :1], right[u_rows, :1], start, width * peers)
        along_v = column_derivative(v, left[v_rows, :1], right[v_rows, :1], start, width * peers)
        source = lax.rem(where_ref[0] + peers - offset, peers)
        lines = pl.ds(pl.multiple_of(source * frames, frames), frames)
        snap_ref[0, lines, :] = along_u.astype(BF16)
        snap_ref[1, lines, :] = slope_v.astype(BF16)
        snap_ref[2, lines, :] = (0.5 * (slope_u + along_v)).astype(BF16)
    pairs = upper_blocks(total // BLOCK)
    half = len(pairs) // 2
    for i in range(total // BLOCK):
        sums = None
        for c in range(3):
            left = snap_ref[c, span(i), :]
            right = snap_ref[c, i * BLOCK:, :]
            part = lax.dot_general(left, right, (((1,), (1,)), ((), ())), preferred_element_type=F32)
            sums = part if sums is None else sums + part
        for n, (line, col) in enumerate(pairs):
            if line == i:
                both_ref[n // half, n % half] = sums[:, (col - i) * BLOCK:(col - i + 1) * BLOCK]
    core = where_ref[3]
    kept_ref[...] = both_ref[core]
    sent_ref[...] = both_ref[1 - core]


def cross_products(where, parts, total):
    width = parts[0].shape[2]
    count = total // BLOCK
    half = count * (count + 1) // 4
    part = jax.ShapeDtypeStruct((half, BLOCK, BLOCK), F32)
    return pl.pallas_call(
        gram_kernel,
        in_specs=[SMEM] + [VMEM] * len(parts),
        out_specs=[VMEM] * 3,
        out_shape=[jax.ShapeDtypeStruct((3, total, width), BF16), part, part],
        scratch_shapes=[pltpu.VMEM((2, half, BLOCK, BLOCK), F32)],
        compiler_params=PARAMS,
        name="gram_kernel",
    )(where, *parts)


def eliminate_block(rows):
    tiles = len(rows)
    lane = lax.broadcasted_iota(jnp.int32, (SUB, BLOCK), 1)
    sub = lax.broadcasted_iota(jnp.int32, (SUB, BLOCK), 0)
    upper, inverse = [], []
    rows = list(rows)
    for step in range(tiles):
        base = step * SUB
        block = rows[step]
        a = {}
        for j in range(SUB):
            column = jnp.broadcast_to(block[:, base + j:base + j + 1], (SUB, BLOCK))
            for i in range(j, SUB):
                a[i, j] = jnp.broadcast_to(column[i:i + 1, :], (SUB, BLOCK))
        inside = (lane >= base) & (lane < base + SUB)
        seeded = jnp.where(inside, (lane - base == sub).astype(F32), block)
        v = [jnp.broadcast_to(seeded[i:i + 1, :], (SUB, BLOCK)) for i in range(SUB)]
        unit = {}
        pivot, root = [], []
        for j in range(SUB):
            inv = 1.0 / a[j, j]
            pivot.append(inv)
            root.append(lax.rsqrt(a[j, j]))
            for i in range(j + 1, SUB):
                unit[i, j] = a[i, j] * inv
            for m in range(j + 1, SUB):
                for i in range(m, SUB):
                    a[i, m] = a[i, m] - (a[i, j] * a[m, j]) * inv
            for i in range(j + 1, SUB):
                v[i] = v[i] - unit[i, j] * v[j]
        z = [v[j] * pivot[j] for j in range(SUB)]
        done = jnp.zeros((SUB, BLOCK), F32)
        corner = jnp.zeros((SUB, BLOCK), F32)
        for i in range(SUB):
            line = jnp.zeros((SUB, BLOCK), F32)
            for m in range(i, SUB):
                line = jnp.where(lane == base + m, a[m, i], line)
            done = jnp.where(sub == i, v[i] * root[i], done)
            corner = jnp.where(sub == i, line * root[i], corner)
        upper.append(jnp.where(lane >= base + SUB, done, corner))
        inverse.append(jnp.where(lane < base + SUB, done, 0.0))
        for q in range(step + 1, tiles):
            old = rows[q]
            acc = jnp.where(inside, 0.0, old)
            left = [jnp.broadcast_to(old[:, base + j:base + j + 1], (SUB, BLOCK)) for j in range(SUB)]
            for j in range(SUB):
                for m in range(j + 1, SUB):
                    left[m] = left[m] - left[j] * unit[m, j]
                acc = acc - left[j] * z[j]
            rows[q] = acc
    return upper, inverse


def span(k):
    return slice(k * BLOCK, (k + 1) * BLOCK)


def factor_kernel(where_ref, kept_ref, other_ref, factor_ref, hi_ref, lo_ref, both_ref, m_ref, t_ref, *, scale):
    n = m_ref.shape[0]
    blocks = n // BLOCK
    core = where_ref[3]
    both_ref[core] = kept_ref[...]
    both_ref[1 - core] = other_ref[...]
    pairs = upper_blocks(blocks)
    half = len(pairs) // 2
    for k in range(1, blocks):
        m_ref[span(k), :k * BLOCK] = jnp.zeros((BLOCK, k * BLOCK), F32)
    for index, (row, col) in enumerate(pairs):
        m_ref[span(row), span(col)] = both_ref[index // half, index % half]
    for k in range(blocks):
        rows = [m_ref[k * BLOCK + s:k * BLOCK + s + SUB, span(k)] for s in range(0, BLOCK, SUB)]
        upper, inverse = eliminate_block(rows)
        for s in range(BLOCK // SUB):
            t_ref[s * SUB:(s + 1) * SUB, :] = inverse[s]
            factor_ref[k * BLOCK + s * SUB:k * BLOCK + (s + 1) * SUB, span(k)] = upper[s] * (1.0 / scale)
        t = t_ref[...]
        m_ref[span(k), :] = lax.dot_general(t, m_ref[span(k), :], (((1,), (0,)), ((), ())), precision=HIGH, preferred_element_type=F32)
        m_ref[span(k), span(k)] = t
        rest = n - (k + 1) * BLOCK
        if rest:
            panel = m_ref[span(k), :]
            below = slice((k + 1) * BLOCK, n)
            m_ref[below, span(k)] = jnp.zeros((rest, BLOCK), F32)
            m_ref[below, :] = m_ref[below, :] - lax.dot_general(panel[:, (k + 1) * BLOCK:], panel, (((0,), (0,)), ((), ())), precision=HIGH, preferred_element_type=F32)
    col = lax.broadcasted_iota(jnp.int32, (BLOCK, n), 1)
    for k in range(blocks):
        whole = m_ref[span(k), :]
        if k + 1 < blocks:
            factor_ref[span(k), (k + 1) * BLOCK:] = whole[:, (k + 1) * BLOCK:] * (1.0 / scale)
        if k:
            factor_ref[span(k), :k * BLOCK] = jnp.zeros((BLOCK, k * BLOCK), F32)
        inv = jnp.where(col < (k + 1) * BLOCK, whole, 0.0) * scale
        hi = inv.astype(BF16)
        hi_ref[span(k), :] = hi
        lo_ref[span(k), :] = (inv - hi.astype(F32)).astype(BF16)


def factorize(where, kept, other, n, scale):
    return pl.pallas_call(
        functools.partial(factor_kernel, scale=scale),
        in_specs=[SMEM, VMEM, VMEM],
        out_specs=[VMEM] * 3,
        out_shape=[jax.ShapeDtypeStruct((n, n), F32)] + [jax.ShapeDtypeStruct((n, n), BF16)] * 2,
        scratch_shapes=[pltpu.VMEM((2,) + kept.shape, F32), pltpu.VMEM((n, n), F32), pltpu.VMEM((BLOCK, BLOCK), F32)],
        compiler_params=PARAMS,
        name="factor_kernel",
    )(where, kept, other)


def basis_kernel(hi_ref, lo_ref, snap_ref, out_ref):
    n = hi_ref.shape[0]
    chunk = n // 2
    for r in range(2):
        rows, depth = slice(r * chunk, (r + 1) * chunk), (r + 1) * chunk
        part = snap_ref[0, :depth, :]
        total = jnp.dot(hi_ref[rows, :depth], part, preferred_element_type=F32)
        total = total + jnp.dot(lo_ref[rows, :depth], part, preferred_element_type=F32)
        out_ref[0, rows, :] = total.astype(BF16)


def make_basis(hi, lo, snap):
    block = pl.BlockSpec((1,) + snap.shape[1:], lambda c: (c, 0, 0))
    return pl.pallas_call(
        basis_kernel,
        grid=(snap.shape[0],),
        in_specs=[VMEM, VMEM, block],
        out_specs=block,
        out_shape=jax.ShapeDtypeStruct(snap.shape, BF16),
        compiler_params=PARAMS,
        name="basis_kernel",
    )(hi, lo, snap)


def sum_devices(kept, sent):
    swap = [(0, 1), (1, 0)]
    shape = kept.shape
    kept = (kept + lax.ppermute(sent, "core", swap)).reshape(-1, shape[-1])
    plane = lax.axis_size(("x", "y"))
    part, width = kept.shape[0] // plane, kept.shape[1]
    piece = lax.all_to_all(kept.reshape(plane, part, width), ("x", "y"), 0, 0, tiled=True).sum(0)
    copies = jnp.broadcast_to(piece[None], (lax.axis_size("z"), part, width))
    piece = lax.all_to_all(copies, "z", 0, 0, tiled=True).sum(0)
    copies = jnp.broadcast_to(piece[None], (plane, part, width))
    kept = lax.all_to_all(copies, ("x", "y"), 0, 0, tiled=True).reshape(shape)
    return kept, lax.ppermute(kept, "core", swap)


def local(displacement):
    frames, _, _, width = displacement.shape
    peers = lax.axis_size("z")
    total_rows = lax.axis_size(TILE)
    total_frames = frames * peers
    scale = math.sqrt(3 * total_rows * width)
    where = jnp.stack([lax.axis_index("z"), lax.axis_index(TILE), jnp.int32(total_rows), lax.axis_index("core")]).astype(jnp.int32)
    planes = displacement.reshape(frames, 2, width).transpose(1, 0, 2)
    first, second = exchange(where, planes, peers)
    up = [(i, i + 1) for i in range(total_rows - 1)]
    down = [(j, i) for i, j in up]
    before = [lax.ppermute(part, TILE, up) for part in (first, second)]
    after = [lax.ppermute(part, TILE, down) for part in (first, second)]
    snap, kept, sent = cross_products(where, [first, second] + before + after, total_frames)
    kept, other = sum_devices(kept, sent)
    factor, hi, lo = factorize(where, kept, other, total_frames, scale)
    basis = make_basis(hi, lo, snap)
    return basis.transpose(1, 0, 2)[:, :, None, :], factor


def solution(mesh):
    frames, tiles = mesh.devices.shape
    side = math.isqrt(tiles // 2)
    split = Mesh(mesh.devices.reshape(frames, side, side, 2), ("z",) + TILE)
    return jax.shard_map(
        local,
        mesh=split,
        in_specs=(P("z", None, TILE, None),),
        out_specs=(P(None, None, TILE, "z"), P()),
        check_vma=False,
    )
```

```python
import functools
import math

import jax
import jax.numpy as jnp
from jax import lax
from jax.experimental import pallas as pl
from jax.experimental.pallas import tpu as pltpu
from jax.sharding import Mesh, PartitionSpec as P

TILE = ("x", "y", "core")
SUB = 8
NEAR = 2
BLOCK = 128
LANES = 128
HIGH = lax.Precision.HIGHEST
F32 = jnp.float32
BF16 = jnp.bfloat16
VMEM = pl.BlockSpec(memory_space=pltpu.VMEM)
SMEM = pl.BlockSpec(memory_space=pltpu.SMEM)
PARAMS = pltpu.CompilerParams(vmem_limit_bytes=24 << 20)


def turns(sign):
    return [0, 2 * sign, -2 * sign, -1, 1, -3, 3, 4]


def spread_kernel(where_ref, planes_ref, *outs):
    place, core = where_ref[0], where_ref[3]
    own_ref, pair_ref = outs[0], outs[1]
    singles = dict(zip((2, 3, 4, 5, 6), outs[2:]))
    width = own_ref.shape[1]
    fields, frames, total = planes_ref.shape
    peers = total // width
    rows = fields * frames
    row = lax.broadcasted_iota(jnp.int32, (SUB, LANES), 0)
    lane = lax.broadcasted_iota(jnp.int32, (SUB, LANES), 1)
    last = ((row == 0) & (lane == LANES - 1)).astype(BF16)
    first = ((row == 1) & (lane == 0)).astype(BF16)
    for slot, offset in enumerate(turns(1 - 2 * core)):
        out_ref = own_ref if slot == 0 else pair_ref.at[0] if slot == 1 else pair_ref.at[1] if slot == 7 else singles[slot]
        start = lax.rem(place + offset + peers, peers) * width
        left = pl.multiple_of(jnp.maximum(start - LANES, 0), LANES)
        right = pl.multiple_of(jnp.minimum(start + width, total - LANES), LANES)
        out_ref[rows:, :] = jnp.zeros((SUB, width), BF16)
        for field in range(fields):
            part = slice(field * frames, (field + 1) * frames)
            out_ref[part, :] = planes_ref[field, :, pl.ds(pl.multiple_of(start, width), width)]
        below = planes_ref[:, :, pl.ds(left, LANES)].reshape(rows, LANES)
        above = planes_ref[:, :, pl.ds(right, LANES)].reshape(rows, LANES)
        dims = (((1,), (1,)), ((), ()))
        edges = lax.dot_general(last, below, dims, preferred_element_type=F32)
        edges = edges + lax.dot_general(first, above, dims, preferred_element_type=F32)
        out_ref[rows:, :rows] = edges.astype(BF16)


def spread(where, planes, peers):
    fields, frames, width = planes.shape
    block = jax.ShapeDtypeStruct((fields * frames + SUB, width // peers), BF16)
    pair = jax.ShapeDtypeStruct((2,) + block.shape, BF16)
    return pl.pallas_call(
        spread_kernel,
        in_specs=[SMEM, VMEM],
        out_specs=[VMEM] * 7,
        out_shape=[block, pair] + [block] * 5,
        compiler_params=PARAMS,
        name="spread_kernel",
    )(where, planes)


def collect_kernel(*refs):
    blocks, out_ref = refs[:-1], refs[-1]
    slot = 0
    for block in blocks:
        if len(block.shape) == 3:
            out_ref[slot] = block[0]
        else:
            out_ref[slot] = block[...]
        slot += 1


def collect(*blocks):
    return pl.pallas_call(
        collect_kernel,
        in_specs=[VMEM] * len(blocks),
        out_specs=VMEM,
        out_shape=jax.ShapeDtypeStruct((len(blocks),) + blocks[0].shape, BF16),
        compiler_params=PARAMS,
        name="collect_kernel",
    )(*blocks)


def shifted(block, near, far, peers):
    pairs = []
    for i in range(peers):
        pairs += [(2 * i, 2 * ((i + near) % peers)), (2 * i + 1, 2 * ((i + far) % peers) + 1)]
    return lax.ppermute(block, ("z", "core"), pairs)


def exchange(where, planes, peers):
    own, pair, back2, minus1, plus1, minus3, plus3 = spread(where, planes, peers)
    pair = shifted(pair, 2, -2, peers)
    back2 = shifted(back2, -2, 2, peers)
    minus1 = shifted(minus1, -1, -1, peers)
    plus1 = shifted(plus1, 1, 1, peers)
    first = collect(own, pair, back2, minus1, plus1)
    minus3 = shifted(minus3, -3, -3, peers)
    plus3 = shifted(plus3, 3, 3, peers)
    relayed = shifted(pair[1], 2, -2, peers)
    second = collect(minus3, plus3, relayed)
    return first, second


NEXT = (0, 2, 1, 3, 4, 5, 6, 7)


def row_derivative(center, before, after, first, final):
    after = jnp.where(final, center, after)
    before = jnp.where(first, center, before)
    return (after - before) * jnp.where(first | final, 1.0, 0.5)


def column_derivative(center, left, right, start, total):
    width = center.shape[1]
    lane = lax.broadcasted_iota(jnp.int32, center.shape, 1)
    column = lane + start
    first, final = column == 0, column == total - 1
    before = jnp.where(lane == 0, left, pltpu.roll(center, 1, 1))
    after = jnp.where(lane == width - 1, right, pltpu.roll(center, width - 1, 1))
    after = jnp.where(final, center, after)
    before = jnp.where(first, center, before)
    return (after - before) * jnp.where(first | final, 1.0, 0.5)


def upper_blocks(count):
    return [(i, j) for i in range(count) for j in range(i, count)]


def gram_kernel(where_ref, *refs):
    parts, snap_ref, kept_ref, sent_ref, both_ref = refs[:6], *refs[6:]
    center, before, after = parts[0:2], parts[2:4], parts[4:6]
    early, _, width = center[0].shape
    peers = early + center[1].shape[0]
    total = snap_ref.shape[1]
    frames = total // peers
    rows = 2 * frames
    top, bottom = where_ref[1] == 0, where_ref[1] == where_ref[2] - 1
    start = where_ref[0] * width
    row = lax.broadcasted_iota(jnp.int32, (SUB, LANES), 0)
    turn = (((0,), (0,)), ((), ()))
    for slot, offset in enumerate(turns(1 - 2 * where_ref[3])):
        chunk, skip = (0, 0) if slot < early else (1, early)
        here = center[chunk].at[slot - skip]
        above = before[chunk].at[NEXT[slot] - skip]
        below = after[chunk].at[NEXT[slot] - skip]
        edges = here[rows:, :rows]
        left = lax.dot_general(edges, (row == 0).astype(BF16), turn, preferred_element_type=F32)
        right = lax.dot_general(edges, (row == 1).astype(BF16), turn, preferred_element_type=F32)
        u_rows, v_rows = slice(0, frames), slice(frames, rows)
        u, v = here[u_rows, :].astype(F32), here[v_rows, :].astype(F32)
        slope_u = row_derivative(u, above[u_rows, :].astype(F32), below[u_rows, :].astype(F32), top, bottom)
        slope_v = row_derivative(v, above[v_rows, :].astype(F32), below[v_rows, :].astype(F32), top, bottom)
        along_u = column_derivative(u, left[u_rows, :1], right[u_rows, :1], start, width * peers)
        along_v = column_derivative(v, left[v_rows, :1], right[v_rows, :1], start, width * peers)
        source = lax.rem(where_ref[0] + peers - offset, peers)
        lines = pl.ds(pl.multiple_of(source * frames, frames), frames)
        snap_ref[0, lines, :] = along_u.astype(BF16)
        snap_ref[1, lines, :] = slope_v.astype(BF16)
        snap_ref[2, lines, :] = (0.5 * (slope_u + along_v)).astype(BF16)
    pairs = upper_blocks(total // BLOCK)
    half = len(pairs) // 2
    for i in range(total // BLOCK):
        sums = None
        for c in range(3):
            left = snap_ref[c, span(i), :]
            right = snap_ref[c, i * BLOCK:, :]
            part = lax.dot_general(left, right, (((1,), (1,)), ((), ())), preferred_element_type=F32)
            sums = part if sums is None else sums + part
        for n, (line, col) in enumerate(pairs):
            if line == i:
                both_ref[n // half, n % half] = sums[:, (col - i) * BLOCK:(col - i + 1) * BLOCK]
    core = where_ref[3]
    kept_ref[...] = both_ref[core]
    sent_ref[...] = both_ref[1 - core]


def cross_products(where, parts, total):
    width = parts[0].shape[2]
    count = total // BLOCK
    half = count * (count + 1) // 4
    part = jax.ShapeDtypeStruct((half, BLOCK, BLOCK), F32)
    return pl.pallas_call(
        gram_kernel,
        in_specs=[SMEM] + [VMEM] * len(parts),
        out_specs=[VMEM] * 3,
        out_shape=[jax.ShapeDtypeStruct((3, total, width), BF16), part, part],
        scratch_shapes=[pltpu.VMEM((2, half, BLOCK, BLOCK), F32)],
        compiler_params=PARAMS,
        name="gram_kernel",
    )(where, *parts)


def split(x):
    top = x.astype(BF16).astype(F32)
    rest = x - top
    middle = rest.astype(BF16).astype(F32)
    return top, middle, rest - middle


LEFT = (0, 0, 1, 1, 0, 2)
RIGHT = (0, 1, 0, 1, 2, 0)
TURNED = (((0,), (0,)), ((), ()))
PLAIN = (((1,), (0,)), ((), ()))


def thin_product(left, right):
    lefts, rights = split(left), split(right)
    lefts = jnp.concatenate([lefts[p] for p in LEFT], 0).astype(BF16)
    rights = jnp.concatenate([rights[p] for p in RIGHT], 0).astype(BF16)
    return lax.dot_general(lefts, rights, TURNED, preferred_element_type=F32)


def long_product(left, right, turned):
    lefts = jnp.concatenate([left[p] for p in LEFT], 0 if turned else 1)
    rights = jnp.concatenate([right[p] for p in RIGHT], 0)
    return lax.dot_general(lefts, rights, TURNED if turned else PLAIN, preferred_element_type=F32)


def eliminate_block(rows, fillers, spread_ref):
    tiles = len(rows)
    lane = lax.broadcasted_iota(jnp.int32, (SUB, BLOCK), 1)
    sub = lax.broadcasted_iota(jnp.int32, (SUB, BLOCK), 0)
    upper, inverse = [], []
    rows = list(rows)
    for step in range(tiles):
        for _ in range(-(-len(fillers) // (tiles - step))):
            fillers.pop(0)()
        base = step * SUB
        block = rows[step]
        a = {}
        for j in range(SUB):
            spread_ref[step % 2, j * SUB:(j + 1) * SUB, :] = jnp.broadcast_to(block[:, base + j:base + j + 1], (SUB, BLOCK))
            for i in range(j, SUB):
                a[i, j] = spread_ref[step % 2, pl.ds(j * SUB + i, SUB, stride=0), :]
        inside = (lane >= base) & (lane < base + SUB)
        seeded = jnp.where(inside, (lane - base == sub).astype(F32), block)
        spread_ref[step % 2, SUB * SUB:, :] = seeded
        v = [spread_ref[step % 2, pl.ds(SUB * SUB + i, SUB, stride=0), :] for i in range(SUB)]
        unit = {}
        pivot, root = [], []
        for j in range(SUB):
            inv = 1.0 / a[j, j]
            pivot.append(inv)
            root.append(lax.rsqrt(a[j, j]))
            for i in range(j + 1, SUB):
                unit[i, j] = a[i, j] * inv
            for m in range(j + 1, SUB):
                for i in range(m, SUB):
                    a[i, m] = a[i, m] - (a[i, j] * a[m, j]) * inv
            for i in range(j + 1, SUB):
                v[i] = v[i] - unit[i, j] * v[j]
        z = [v[j] * pivot[j] for j in range(SUB)]
        done = jnp.zeros((SUB, BLOCK), F32)
        corner = jnp.zeros((SUB, BLOCK), F32)
        for i in range(SUB):
            line = jnp.zeros((SUB, BLOCK), F32)
            for m in range(i, SUB):
                line = jnp.where(lane == base + m, a[m, i], line)
            done = jnp.where(sub == i, v[i] * root[i], done)
            corner = jnp.where(sub == i, line * root[i], corner)
        upper.append(jnp.where(lane >= base + SUB, done, corner))
        inverse.append(jnp.where(lane < base + SUB, done, 0.0))
        for q in range(step + 1, min(step + 1 + NEAR, tiles)):
            old = rows[q]
            acc = jnp.where(inside, 0.0, old)
            left = [jnp.broadcast_to(old[:, base + j:base + j + 1], (SUB, BLOCK)) for j in range(SUB)]
            for j in range(SUB):
                for m in range(j + 1, SUB):
                    left[m] = left[m] - left[j] * unit[m, j]
                acc = acc - left[j] * z[j]
            rows[q] = acc
        if step + 1 + NEAR < tiles:
            update = thin_product(done, done)
            for q in range(step + 1 + NEAR, tiles):
                rows[q] = jnp.where(inside, 0.0, rows[q]) - update[q * SUB:(q + 1) * SUB, :]
    return upper, inverse


def span(k):
    return slice(k * BLOCK, (k + 1) * BLOCK)


def factor_kernel(where_ref, kept_ref, other_ref, snap_ref, factor_hbm, basis_hbm, gram_ref, carry_ref, part_ref, factor_ref, basis_ref, spread_ref, sems, *, scale):
    n = factor_ref.shape[0]
    blocks = n // BLOCK
    core = where_ref[3]
    gram_ref[core] = kept_ref[...]
    gram_ref[1 - core] = other_ref[...]
    place = {pair: index for index, pair in enumerate(upper_blocks(blocks))}
    half = len(place) // 2

    def gram(i, m):
        return gram_ref.at[place[i, m] // half, place[i, m] % half]

    def carried(i, j):
        return carry_ref.at[i * (i - 1) // 2 + j]

    def parts(k, m):
        return [part_ref[k, p, :, span(m)] for p in range(3)]

    def keep(k, m, value):
        for p, part in enumerate(split(value)):
            part_ref[k, p, :, span(m)] = part.astype(BF16)

    def upper_panel(k, m):
        value = long_product(parts(k, k), split_block(gram(k, m)[...]), False)
        factor_ref[span(k), span(m)] = value * (1.0 / scale)
        keep(k, m, value)

    def split_block(value):
        return [part.astype(BF16) for part in split(value)]

    def update_gram(k, i, m):
        ref = gram(i, m)
        ref[...] = ref[...] - long_product(parts(k, i), parts(k, m), True)

    def update_carried(k, i, j):
        ref = carried(i, j)
        product = long_product(parts(k, i), parts(k, j), True)
        ref[...] = -product if j == k else ref[...] - product

    def lower_panel(k, j):
        keep(k, j, long_product(parts(k, k), split_block(carried(k, j)[...]), False))

    def basis_rows(k, c):
        depth = (k + 1) * BLOCK
        snap = snap_ref[c, :depth, :]
        total = jnp.dot(part_ref[k, 0, :, :depth], snap, preferred_element_type=F32)
        total = total + jnp.dot(part_ref[k, 1, :, :depth], snap, preferred_element_type=F32)
        basis_ref[c, span(k), :] = (total * scale).astype(BF16)

    def copies(k):
        return (
            pltpu.make_async_copy(basis_ref.at[:, span(k), :], basis_hbm.at[:, span(k), :], sems.at[0, k]),
            pltpu.make_async_copy(factor_ref.at[span(k), :], factor_hbm.at[span(k), :], sems.at[1, k]),
        )

    def send(k):
        for copy in copies(k):
            copy.start()

    fillers = []
    for k in range(blocks):
        diagonal = gram(k, k)
        rows = [diagonal[s:s + SUB, :] for s in range(0, BLOCK, SUB)]
        upper, inverse = eliminate_block(rows, fillers, spread_ref)
        keep(k, k, jnp.concatenate(inverse, 0))
        factor_ref[span(k), span(k)] = jnp.concatenate(upper, 0) * (1.0 / scale)
        if k:
            factor_ref[span(k), :k * BLOCK] = jnp.zeros((BLOCK, k * BLOCK), F32)
        later = range(k + 1, blocks)
        if later:
            upper_panel(k, k + 1)
            update_gram(k, k + 1, k + 1)
        fillers = [functools.partial(upper_panel, k, m) for m in later[1:]]
        fillers += [functools.partial(lower_panel, k, j) for j in range(k)]
        fillers += [functools.partial(update_gram, k, i, m) for i in later for m in range(i, blocks) if (i, m) != (k + 1, k + 1)]
        fillers += [functools.partial(update_carried, k, i, j) for i in later for j in range(k + 1)]
        fillers += [functools.partial(basis_rows, k, c) for c in range(snap_ref.shape[0])]
        fillers.append(functools.partial(send, k))
    for filler in fillers:
        filler()
    for k in range(blocks):
        for copy in copies(k):
            copy.wait()


def factorize(where, kept, other, snap, scale):
    n = snap.shape[1]
    blocks = n // BLOCK
    return pl.pallas_call(
        functools.partial(factor_kernel, scale=scale),
        in_specs=[SMEM, VMEM, VMEM, VMEM],
        out_specs=[pl.BlockSpec(memory_space=pl.ANY)] * 2,
        out_shape=[jax.ShapeDtypeStruct((n, n), F32), jax.ShapeDtypeStruct(snap.shape, BF16)],
        scratch_shapes=[
            pltpu.VMEM((2,) + kept.shape, F32),
            pltpu.VMEM((blocks * (blocks - 1) // 2, BLOCK, BLOCK), F32),
            pltpu.VMEM((blocks, 3, BLOCK, n), BF16),
            pltpu.VMEM((n, n), F32),
            pltpu.VMEM(snap.shape, BF16),
            pltpu.VMEM((2, SUB * (SUB + 1), BLOCK), F32),
            pltpu.SemaphoreType.DMA((2, blocks)),
        ],
        compiler_params=PARAMS,
        name="factor_kernel",
    )(where, kept, other, snap)


def sum_devices(kept, sent):
    swap = [(0, 1), (1, 0)]
    shape = kept.shape
    kept = (kept + lax.ppermute(sent, "core", swap)).reshape(-1, shape[-1])
    plane = lax.axis_size(("x", "y"))
    part, width = kept.shape[0] // plane, kept.shape[1]
    piece = lax.all_to_all(kept.reshape(plane, part, width), ("x", "y"), 0, 0, tiled=True).sum(0)
    copies = jnp.broadcast_to(piece[None], (lax.axis_size("z"), part, width))
    piece = lax.all_to_all(copies, "z", 0, 0, tiled=True).sum(0)
    copies = jnp.broadcast_to(piece[None], (plane, part, width))
    kept = lax.all_to_all(copies, ("x", "y"), 0, 0, tiled=True).reshape(shape)
    return kept, lax.ppermute(kept, "core", swap)


def local(displacement):
    frames, _, _, width = displacement.shape
    peers = lax.axis_size("z")
    total_rows = lax.axis_size(TILE)
    total_frames = frames * peers
    scale = math.sqrt(3 * total_rows * width)
    where = jnp.stack([lax.axis_index("z"), lax.axis_index(TILE), jnp.int32(total_rows), lax.axis_index("core")]).astype(jnp.int32)
    planes = displacement.reshape(frames, 2, width).transpose(1, 0, 2)
    first, second = exchange(where, planes, peers)
    up = [(i, i + 1) for i in range(total_rows - 1)]
    down = [(j, i) for i, j in up]
    before = [lax.ppermute(part, TILE, up) for part in (first, second)]
    after = [lax.ppermute(part, TILE, down) for part in (first, second)]
    snap, kept, sent = cross_products(where, [first, second] + before + after, total_frames)
    kept, other = sum_devices(kept, sent)
    factor, basis = factorize(where, kept, other, snap, scale)
    return basis.transpose(1, 0, 2)[:, :, None, :], factor


def solution(mesh):
    frames, tiles = mesh.devices.shape
    side = math.isqrt(tiles // 2)
    split = Mesh(mesh.devices.reshape(frames, side, side, 2), ("z",) + TILE)
    return jax.shard_map(
        local,
        mesh=split,
        in_specs=(P("z", None, TILE, None),),
        out_specs=(P(None, None, TILE, "z"), P()),
        check_vma=False,
    )
```

```python
import functools
import math

import jax
import jax.numpy as jnp
from jax import lax
from jax.experimental import pallas as pl
from jax.experimental.pallas import tpu as pltpu
from jax.sharding import Mesh, PartitionSpec as P

TILE = ("x", "y", "core")
SUB = 8
NEAR = 2
BLOCK = 128
LANES = 128
HIGH = lax.Precision.HIGHEST
F32 = jnp.float32
BF16 = jnp.bfloat16
VMEM = pl.BlockSpec(memory_space=pltpu.VMEM)
SMEM = pl.BlockSpec(memory_space=pltpu.SMEM)
PARAMS = pltpu.CompilerParams(vmem_limit_bytes=24 << 20)


def turns(sign):
    return [0, 2 * sign, -2 * sign, -1, 1, -3, 3, 4]


def spread_kernel(where_ref, planes_ref, *outs):
    place, core = where_ref[0], where_ref[3]
    own_ref, pair_ref = outs[0], outs[1]
    singles = dict(zip((2, 3, 4, 5, 6), outs[2:]))
    width = own_ref.shape[1]
    fields, frames, total = planes_ref.shape
    peers = total // width
    rows = fields * frames
    row = lax.broadcasted_iota(jnp.int32, (SUB, LANES), 0)
    lane = lax.broadcasted_iota(jnp.int32, (SUB, LANES), 1)
    last = ((row == 0) & (lane == LANES - 1)).astype(BF16)
    first = ((row == 1) & (lane == 0)).astype(BF16)
    for slot, offset in enumerate(turns(1 - 2 * core)):
        out_ref = own_ref if slot == 0 else pair_ref.at[0] if slot == 1 else pair_ref.at[1] if slot == 7 else singles[slot]
        start = lax.rem(place + offset + peers, peers) * width
        left = pl.multiple_of(jnp.maximum(start - LANES, 0), LANES)
        right = pl.multiple_of(jnp.minimum(start + width, total - LANES), LANES)
        out_ref[rows:, :] = jnp.zeros((SUB, width), BF16)
        for field in range(fields):
            part = slice(field * frames, (field + 1) * frames)
            out_ref[part, :] = planes_ref[field, :, pl.ds(pl.multiple_of(start, width), width)]
        below = planes_ref[:, :, pl.ds(left, LANES)].reshape(rows, LANES)
        above = planes_ref[:, :, pl.ds(right, LANES)].reshape(rows, LANES)
        dims = (((1,), (1,)), ((), ()))
        edges = lax.dot_general(last, below, dims, preferred_element_type=F32)
        edges = edges + lax.dot_general(first, above, dims, preferred_element_type=F32)
        out_ref[rows:, :rows] = edges.astype(BF16)


def spread(where, planes, peers):
    fields, frames, width = planes.shape
    block = jax.ShapeDtypeStruct((fields * frames + SUB, width // peers), BF16)
    pair = jax.ShapeDtypeStruct((2,) + block.shape, BF16)
    return pl.pallas_call(
        spread_kernel,
        in_specs=[SMEM, VMEM],
        out_specs=[VMEM] * 7,
        out_shape=[block, pair] + [block] * 5,
        compiler_params=PARAMS,
        name="spread_kernel",
    )(where, planes)


def collect_kernel(*refs):
    blocks, out_ref = refs[:-1], refs[-1]
    slot = 0
    for block in blocks:
        if len(block.shape) == 3:
            out_ref[slot] = block[0]
        else:
            out_ref[slot] = block[...]
        slot += 1


def collect(*blocks):
    return pl.pallas_call(
        collect_kernel,
        in_specs=[VMEM] * len(blocks),
        out_specs=VMEM,
        out_shape=jax.ShapeDtypeStruct((len(blocks),) + blocks[0].shape, BF16),
        compiler_params=PARAMS,
        name="collect_kernel",
    )(*blocks)


def shifted(block, near, far, peers):
    pairs = []
    for i in range(peers):
        pairs += [(2 * i, 2 * ((i + near) % peers)), (2 * i + 1, 2 * ((i + far) % peers) + 1)]
    return lax.ppermute(block, ("z", "core"), pairs)


def exchange(where, planes, peers):
    own, pair, back2, minus1, plus1, minus3, plus3 = spread(where, planes, peers)
    pair = shifted(pair, 2, -2, peers)
    back2 = shifted(back2, -2, 2, peers)
    minus1 = shifted(minus1, -1, -1, peers)
    plus1 = shifted(plus1, 1, 1, peers)
    first = collect(own, pair, back2, minus1, plus1)
    minus3 = shifted(minus3, -3, -3, peers)
    plus3 = shifted(plus3, 3, 3, peers)
    relayed = shifted(pair[1], 2, -2, peers)
    second = collect(minus3, plus3, relayed)
    return first, second


NEXT = (0, 2, 1, 3, 4, 5, 6, 7)


def row_derivative(center, inner, outer, edge, factor):
    return (inner - jnp.where(edge, center, outer)) * factor


def column_derivative(center, left, right, start, total):
    width = center.shape[1]
    lane = lax.broadcasted_iota(jnp.int32, center.shape, 1)
    column = lane + start
    first, final = column == 0, column == total - 1
    before = jnp.where(lane == 0, left, pltpu.roll(center, 1, 1))
    after = jnp.where(lane == width - 1, right, pltpu.roll(center, width - 1, 1))
    after = jnp.where(final, center, after)
    before = jnp.where(first, center, before)
    return (after - before) * jnp.where(first | final, 1.0, 0.5)


def upper_blocks(count):
    return [(i, j) for i in range(count) for j in range(i, count)]


def gram_kernel(where_ref, *refs):
    parts, snap_ref, kept_ref, sent_ref, both_ref = refs[:6], *refs[6:]
    center, inner, outer = parts[0:2], parts[2:4], parts[4:6]
    early, _, width = center[0].shape
    peers = early + center[1].shape[0]
    total = snap_ref.shape[1]
    frames = total // peers
    rows = 2 * frames
    edge = (where_ref[1] == 0) | (where_ref[1] == where_ref[2] - 1)
    factor = jnp.where(edge, 1.0, 0.5) * jnp.where(where_ref[3] == 0, 1.0, -1.0)
    start = where_ref[0] * width
    row = lax.broadcasted_iota(jnp.int32, (SUB, LANES), 0)
    turn = (((0,), (0,)), ((), ()))
    for slot, offset in enumerate(turns(1 - 2 * where_ref[3])):
        chunk, skip = (0, 0) if slot < early else (1, early)
        here = center[chunk].at[slot - skip]
        near = inner[chunk].at[NEXT[slot] - skip]
        far = outer[chunk].at[NEXT[slot] - skip]
        edges = here[rows:, :rows]
        left = lax.dot_general(edges, (row == 0).astype(BF16), turn, preferred_element_type=F32)
        right = lax.dot_general(edges, (row == 1).astype(BF16), turn, preferred_element_type=F32)
        u_rows, v_rows = slice(0, frames), slice(frames, rows)
        u, v = here[u_rows, :].astype(F32), here[v_rows, :].astype(F32)
        slope_u = row_derivative(u, near[u_rows, :].astype(F32), far[u_rows, :].astype(F32), edge, factor)
        slope_v = row_derivative(v, near[v_rows, :].astype(F32), far[v_rows, :].astype(F32), edge, factor)
        along_u = column_derivative(u, left[u_rows, :1], right[u_rows, :1], start, width * peers)
        along_v = column_derivative(v, left[v_rows, :1], right[v_rows, :1], start, width * peers)
        source = lax.rem(where_ref[0] + peers - offset, peers)
        lines = pl.ds(pl.multiple_of(source * frames, frames), frames)
        snap_ref[0, lines, :] = along_u.astype(BF16)
        snap_ref[1, lines, :] = slope_v.astype(BF16)
        snap_ref[2, lines, :] = (0.5 * (slope_u + along_v)).astype(BF16)
    pairs = upper_blocks(total // BLOCK)
    half = len(pairs) // 2
    for i in range(total // BLOCK):
        sums = None
        for c in range(3):
            left = snap_ref[c, span(i), :]
            right = snap_ref[c, i * BLOCK:, :]
            part = lax.dot_general(left, right, (((1,), (1,)), ((), ())), preferred_element_type=F32)
            sums = part if sums is None else sums + part
        for n, (line, col) in enumerate(pairs):
            if line == i:
                both_ref[n // half, n % half] = sums[:, (col - i) * BLOCK:(col - i + 1) * BLOCK]
    core = where_ref[3]
    kept_ref[...] = both_ref[core]
    sent_ref[...] = both_ref[1 - core]


def cross_products(where, parts, total):
    width = parts[0].shape[2]
    count = total // BLOCK
    half = count * (count + 1) // 4
    part = jax.ShapeDtypeStruct((half, BLOCK, BLOCK), F32)
    return pl.pallas_call(
        gram_kernel,
        in_specs=[SMEM] + [VMEM] * len(parts),
        out_specs=[VMEM] * 3,
        out_shape=[jax.ShapeDtypeStruct((3, total, width), BF16), part, part],
        scratch_shapes=[pltpu.VMEM((2, half, BLOCK, BLOCK), F32)],
        compiler_params=PARAMS,
        name="gram_kernel",
    )(where, *parts)


def split(x):
    top = x.astype(BF16).astype(F32)
    rest = x - top
    middle = rest.astype(BF16).astype(F32)
    return top, middle, rest - middle


LEFT = (0, 0, 1, 1, 0, 2)
RIGHT = (0, 1, 0, 1, 2, 0)
TURNED = (((0,), (0,)), ((), ()))
PLAIN = (((1,), (0,)), ((), ()))


def thin_product(left, right):
    lefts, rights = split(left), split(right)
    lefts = jnp.concatenate([lefts[p] for p in LEFT], 0).astype(BF16)
    rights = jnp.concatenate([rights[p] for p in RIGHT], 0).astype(BF16)
    return lax.dot_general(lefts, rights, TURNED, preferred_element_type=F32)


def long_product(left, right, turned):
    lefts = jnp.concatenate([left[p] for p in LEFT], 0 if turned else 1)
    rights = jnp.concatenate([right[p] for p in RIGHT], 0)
    return lax.dot_general(lefts, rights, TURNED if turned else PLAIN, preferred_element_type=F32)


def eliminate_block(rows, fillers, spread_ref):
    tiles = len(rows)
    lane = lax.broadcasted_iota(jnp.int32, (SUB, BLOCK), 1)
    sub = lax.broadcasted_iota(jnp.int32, (SUB, BLOCK), 0)
    upper, inverse = [], []
    rows = list(rows)
    for step in range(tiles):
        for _ in range(-(-len(fillers) // (tiles - step))):
            fillers.pop(0)()
        base = step * SUB
        block = rows[step]
        a = {}
        for j in range(SUB):
            spread_ref[step % 2, j * SUB:(j + 1) * SUB, :] = jnp.broadcast_to(block[:, base + j:base + j + 1], (SUB, BLOCK))
            for i in range(j, SUB):
                a[i, j] = spread_ref[step % 2, pl.ds(j * SUB + i, SUB, stride=0), :]
        inside = (lane >= base) & (lane < base + SUB)
        seeded = jnp.where(inside, (lane - base == sub).astype(F32), block)
        spread_ref[step % 2, SUB * SUB:, :] = seeded
        v = [spread_ref[step % 2, pl.ds(SUB * SUB + i, SUB, stride=0), :] for i in range(SUB)]
        unit = {}
        pivot, root = [], []
        for j in range(SUB):
            inv = 1.0 / a[j, j]
            pivot.append(inv)
            root.append(lax.rsqrt(a[j, j]))
            for i in range(j + 1, SUB):
                unit[i, j] = a[i, j] * inv
            for m in range(j + 1, SUB):
                for i in range(m, SUB):
                    a[i, m] = a[i, m] - (a[i, j] * a[m, j]) * inv
            for i in range(j + 1, SUB):
                v[i] = v[i] - unit[i, j] * v[j]
        z = [v[j] * pivot[j] for j in range(SUB)]
        done = jnp.zeros((SUB, BLOCK), F32)
        corner = jnp.zeros((SUB, BLOCK), F32)
        for i in range(SUB):
            line = jnp.zeros((SUB, BLOCK), F32)
            for m in range(i, SUB):
                line = jnp.where(lane == base + m, a[m, i], line)
            done = jnp.where(sub == i, v[i] * root[i], done)
            corner = jnp.where(sub == i, line * root[i], corner)
        upper.append(jnp.where(lane >= base + SUB, done, corner))
        inverse.append(jnp.where(lane < base + SUB, done, 0.0))
        for q in range(step + 1, min(step + 1 + NEAR, tiles)):
            old = rows[q]
            acc = jnp.where(inside, 0.0, old)
            left = [jnp.broadcast_to(old[:, base + j:base + j + 1], (SUB, BLOCK)) for j in range(SUB)]
            for j in range(SUB):
                for m in range(j + 1, SUB):
                    left[m] = left[m] - left[j] * unit[m, j]
                acc = acc - left[j] * z[j]
            rows[q] = acc
        if step + 1 + NEAR < tiles:
            update = thin_product(done, done)
            for q in range(step + 1 + NEAR, tiles):
                rows[q] = jnp.where(inside, 0.0, rows[q]) - update[q * SUB:(q + 1) * SUB, :]
    return upper, inverse


def span(k):
    return slice(k * BLOCK, (k + 1) * BLOCK)


def factor_kernel(where_ref, kept_ref, other_ref, snap_ref, factor_hbm, basis_hbm, gram_ref, carry_ref, part_ref, factor_ref, basis_ref, spread_ref, sems, *, scale):
    n = factor_ref.shape[0]
    blocks = n // BLOCK
    core = where_ref[3]
    gram_ref[core] = kept_ref[...]
    gram_ref[1 - core] = other_ref[...]
    place = {pair: index for index, pair in enumerate(upper_blocks(blocks))}
    half = len(place) // 2

    def gram(i, m):
        return gram_ref.at[place[i, m] // half, place[i, m] % half]

    def carried(i, j):
        return carry_ref.at[i * (i - 1) // 2 + j]

    def parts(k, m):
        return [part_ref[k, p, :, span(m)] for p in range(3)]

    def keep(k, m, value):
        for p, part in enumerate(split(value)):
            part_ref[k, p, :, span(m)] = part.astype(BF16)

    def upper_panel(k, m):
        value = long_product(parts(k, k), split_block(gram(k, m)[...]), False)
        factor_ref[span(k), span(m)] = value * (1.0 / scale)
        keep(k, m, value)

    def split_block(value):
        return [part.astype(BF16) for part in split(value)]

    def update_gram(k, i, m):
        ref = gram(i, m)
        ref[...] = ref[...] - long_product(parts(k, i), parts(k, m), True)

    def update_carried(k, i, j):
        ref = carried(i, j)
        product = long_product(parts(k, i), parts(k, j), True)
        ref[...] = -product if j == k else ref[...] - product

    def lower_panel(k, j):
        keep(k, j, long_product(parts(k, k), split_block(carried(k, j)[...]), False))

    def basis_rows(k, c):
        depth = (k + 1) * BLOCK
        snap = snap_ref[c, :depth, :]
        total = jnp.dot(part_ref[k, 0, :, :depth], snap, preferred_element_type=F32)
        total = total + jnp.dot(part_ref[k, 1, :, :depth], snap, preferred_element_type=F32)
        basis_ref[c, span(k), :] = (total * scale).astype(BF16)

    def copies(k):
        return (
            pltpu.make_async_copy(basis_ref.at[:, span(k), :], basis_hbm.at[:, span(k), :], sems.at[0, k]),
            pltpu.make_async_copy(factor_ref.at[span(k), :], factor_hbm.at[span(k), :], sems.at[1, k]),
        )

    def send(k):
        for copy in copies(k):
            copy.start()

    fillers = []
    for k in range(blocks):
        diagonal = gram(k, k)
        rows = [diagonal[s:s + SUB, :] for s in range(0, BLOCK, SUB)]
        upper, inverse = eliminate_block(rows, fillers, spread_ref)
        keep(k, k, jnp.concatenate(inverse, 0))
        factor_ref[span(k), span(k)] = jnp.concatenate(upper, 0) * (1.0 / scale)
        if k:
            factor_ref[span(k), :k * BLOCK] = jnp.zeros((BLOCK, k * BLOCK), F32)
        later = range(k + 1, blocks)
        if later:
            upper_panel(k, k + 1)
            update_gram(k, k + 1, k + 1)
        fillers = [functools.partial(upper_panel, k, m) for m in later[1:]]
        fillers += [functools.partial(lower_panel, k, j) for j in range(k)]
        fillers += [functools.partial(update_gram, k, i, m) for i in later for m in range(i, blocks) if (i, m) != (k + 1, k + 1)]
        fillers += [functools.partial(update_carried, k, i, j) for i in later for j in range(k + 1)]
        fillers += [functools.partial(basis_rows, k, c) for c in range(snap_ref.shape[0])]
        fillers.append(functools.partial(send, k))
    for filler in fillers:
        filler()
    for k in range(blocks):
        for copy in copies(k):
            copy.wait()


def factorize(where, kept, other, snap, scale):
    n = snap.shape[1]
    blocks = n // BLOCK
    return pl.pallas_call(
        functools.partial(factor_kernel, scale=scale),
        in_specs=[SMEM, VMEM, VMEM, VMEM],
        out_specs=[pl.BlockSpec(memory_space=pl.ANY)] * 2,
        out_shape=[jax.ShapeDtypeStruct((n, n), F32), jax.ShapeDtypeStruct(snap.shape, BF16)],
        scratch_shapes=[
            pltpu.VMEM((2,) + kept.shape, F32),
            pltpu.VMEM((blocks * (blocks - 1) // 2, BLOCK, BLOCK), F32),
            pltpu.VMEM((blocks, 3, BLOCK, n), BF16),
            pltpu.VMEM((n, n), F32),
            pltpu.VMEM(snap.shape, BF16),
            pltpu.VMEM((2, SUB * (SUB + 1), BLOCK), F32),
            pltpu.SemaphoreType.DMA((2, blocks)),
        ],
        compiler_params=PARAMS,
        name="factor_kernel",
    )(where, kept, other, snap)


def sum_devices(kept, sent):
    swap = [(0, 1), (1, 0)]
    shape = kept.shape
    kept = (kept + lax.ppermute(sent, "core", swap)).reshape(-1, shape[-1])
    plane = lax.axis_size(("x", "y"))
    part, width = kept.shape[0] // plane, kept.shape[1]
    piece = lax.all_to_all(kept.reshape(plane, part, width), ("x", "y"), 0, 0, tiled=True).sum(0)
    copies = jnp.broadcast_to(piece[None], (lax.axis_size("z"), part, width))
    piece = lax.all_to_all(copies, "z", 0, 0, tiled=True).sum(0)
    copies = jnp.broadcast_to(piece[None], (plane, part, width))
    kept = lax.all_to_all(copies, ("x", "y"), 0, 0, tiled=True).reshape(shape)
    return kept, lax.ppermute(kept, "core", swap)


def local(displacement):
    frames, _, _, width = displacement.shape
    peers = lax.axis_size("z")
    total_rows = lax.axis_size(TILE)
    total_frames = frames * peers
    scale = math.sqrt(3 * total_rows * width)
    where = jnp.stack([lax.axis_index("z"), lax.axis_index(TILE), jnp.int32(total_rows), lax.axis_index("core")]).astype(jnp.int32)
    planes = displacement.reshape(frames, 2, width).transpose(1, 0, 2)
    first, second = exchange(where, planes, peers)
    chip = [(i, i ^ 1) for i in range(total_rows)]
    between = [(i, ((i + 1) ^ 1) - 1) for i in range(1, total_rows - 1)]
    inner = [lax.ppermute(part, TILE, chip) for part in (first, second)]
    outer = [lax.ppermute(part, TILE, between) for part in (first, second)]
    snap, kept, sent = cross_products(where, [first, second] + inner + outer, total_frames)
    kept, other = sum_devices(kept, sent)
    factor, basis = factorize(where, kept, other, snap, scale)
    return basis.transpose(1, 0, 2)[:, :, None, :], factor


def solution(mesh):
    frames, tiles = mesh.devices.shape
    side = math.isqrt(tiles // 2)
    split = Mesh(mesh.devices.reshape(frames, side, side, 2), ("z",) + TILE)
    return jax.shard_map(
        local,
        mesh=split,
        in_specs=(P("z", None, TILE, None),),
        out_specs=(P(None, None, TILE, "z"), P()),
        check_vma=False,
    )
```

```python
import functools
import math

import jax
import jax.numpy as jnp
from jax import lax
from jax.experimental import pallas as pl
from jax.experimental.pallas import tpu as pltpu
from jax.sharding import Mesh, PartitionSpec as P

TILE = ("x", "y", "core")
SUB = 8
NEAR = 2
BLOCK = 128
LANES = 128
HIGH = lax.Precision.HIGHEST
F32 = jnp.float32
BF16 = jnp.bfloat16
VMEM = pl.BlockSpec(memory_space=pltpu.VMEM)
SMEM = pl.BlockSpec(memory_space=pltpu.SMEM)
PARAMS = pltpu.CompilerParams(vmem_limit_bytes=24 << 20)


def turns(sign):
    return [0, 2 * sign, -2 * sign, -1, 1, -3, 3, 4]


def spread_kernel(where_ref, planes_ref, *outs):
    place, core = where_ref[0], where_ref[3]
    own_ref, pair_ref = outs[0], outs[1]
    singles = dict(zip((2, 3, 4, 5, 6), outs[2:]))
    width = own_ref.shape[1]
    fields, frames, total = planes_ref.shape
    peers = total // width
    rows = fields * frames
    row = lax.broadcasted_iota(jnp.int32, (SUB, LANES), 0)
    lane = lax.broadcasted_iota(jnp.int32, (SUB, LANES), 1)
    last = ((row == 0) & (lane == LANES - 1)).astype(BF16)
    first = ((row == 1) & (lane == 0)).astype(BF16)
    for slot, offset in enumerate(turns(1 - 2 * core)):
        out_ref = own_ref if slot == 0 else pair_ref.at[0] if slot == 1 else pair_ref.at[1] if slot == 7 else singles[slot]
        start = lax.rem(place + offset + peers, peers) * width
        left = pl.multiple_of(jnp.maximum(start - LANES, 0), LANES)
        right = pl.multiple_of(jnp.minimum(start + width, total - LANES), LANES)
        out_ref[rows:, :] = jnp.zeros((SUB, width), BF16)
        for field in range(fields):
            part = slice(field * frames, (field + 1) * frames)
            out_ref[part, :] = planes_ref[field, :, pl.ds(pl.multiple_of(start, width), width)]
        below = planes_ref[:, :, pl.ds(left, LANES)].reshape(rows, LANES)
        above = planes_ref[:, :, pl.ds(right, LANES)].reshape(rows, LANES)
        dims = (((1,), (1,)), ((), ()))
        edges = lax.dot_general(last, below, dims, preferred_element_type=F32)
        edges = edges + lax.dot_general(first, above, dims, preferred_element_type=F32)
        out_ref[rows:, :rows] = edges.astype(BF16)


def spread(where, planes, peers):
    fields, frames, width = planes.shape
    block = jax.ShapeDtypeStruct((fields * frames + SUB, width // peers), BF16)
    pair = jax.ShapeDtypeStruct((2,) + block.shape, BF16)
    return pl.pallas_call(
        spread_kernel,
        in_specs=[SMEM, VMEM],
        out_specs=[VMEM] * 7,
        out_shape=[block, pair] + [block] * 5,
        compiler_params=PARAMS,
        name="spread_kernel",
    )(where, planes)


def collect_kernel(*refs):
    blocks, out_ref = refs[:-1], refs[-1]
    slot = 0
    for block in blocks:
        if len(block.shape) == 3:
            out_ref[slot] = block[0]
        else:
            out_ref[slot] = block[...]
        slot += 1


def collect(*blocks):
    return pl.pallas_call(
        collect_kernel,
        in_specs=[VMEM] * len(blocks),
        out_specs=VMEM,
        out_shape=jax.ShapeDtypeStruct((len(blocks),) + blocks[0].shape, BF16),
        compiler_params=PARAMS,
        name="collect_kernel",
    )(*blocks)


def shifted(block, near, far, peers):
    pairs = []
    for i in range(peers):
        pairs += [(2 * i, 2 * ((i + near) % peers)), (2 * i + 1, 2 * ((i + far) % peers) + 1)]
    return lax.ppermute(block, ("z", "core"), pairs)


def exchange(where, planes, peers):
    own, pair, back2, minus1, plus1, minus3, plus3 = spread(where, planes, peers)
    pair = shifted(pair, 2, -2, peers)
    back2 = shifted(back2, -2, 2, peers)
    minus1 = shifted(minus1, -1, -1, peers)
    plus1 = shifted(plus1, 1, 1, peers)
    first = collect(own, pair, back2, minus1, plus1)
    minus3 = shifted(minus3, -3, -3, peers)
    plus3 = shifted(plus3, 3, 3, peers)
    relayed = shifted(pair[1], 2, -2, peers)
    second = collect(minus3, plus3, relayed)
    return first, second


NEXT = (0, 2, 1, 3, 4, 5, 6, 7)


def row_derivative(center, inner, outer, edge, factor):
    return (inner - jnp.where(edge, center, outer)) * factor


def column_derivative(center, left, right, start, total):
    width = center.shape[1]
    lane = lax.broadcasted_iota(jnp.int32, center.shape, 1)
    column = lane + start
    first, final = column == 0, column == total - 1
    before = jnp.where(lane == 0, left, pltpu.roll(center, 1, 1))
    after = jnp.where(lane == width - 1, right, pltpu.roll(center, width - 1, 1))
    after = jnp.where(final, center, after)
    before = jnp.where(first, center, before)
    return (after - before) * jnp.where(first | final, 1.0, 0.5)


def upper_blocks(count):
    return [(i, j) for i in range(count) for j in range(i, count)]


def gram_kernel(where_ref, *refs):
    parts, snap_ref, kept_ref, sent_ref, both_ref = refs[:6], *refs[6:]
    center, inner, outer = parts[0:2], parts[2:4], parts[4:6]
    early, _, width = center[0].shape
    peers = early + center[1].shape[0]
    total = snap_ref.shape[1]
    frames = total // peers
    rows = 2 * frames
    edge = (where_ref[1] == 0) | (where_ref[1] == where_ref[2] - 1)
    factor = jnp.where(edge, 1.0, 0.5) * jnp.where(where_ref[3] == 0, 1.0, -1.0)
    start = where_ref[0] * width
    row = lax.broadcasted_iota(jnp.int32, (SUB, LANES), 0)
    turn = (((0,), (0,)), ((), ()))
    for slot, offset in enumerate(turns(1 - 2 * where_ref[3])):
        chunk, skip = (0, 0) if slot < early else (1, early)
        here = center[chunk].at[slot - skip]
        near = inner[chunk].at[NEXT[slot] - skip]
        far = outer[chunk].at[NEXT[slot] - skip]
        edges = here[rows:, :rows]
        left = lax.dot_general(edges, (row == 0).astype(BF16), turn, preferred_element_type=F32)
        right = lax.dot_general(edges, (row == 1).astype(BF16), turn, preferred_element_type=F32)
        u_rows, v_rows = slice(0, frames), slice(frames, rows)
        u, v = here[u_rows, :].astype(F32), here[v_rows, :].astype(F32)
        slope_u = row_derivative(u, near[u_rows, :].astype(F32), far[u_rows, :].astype(F32), edge, factor)
        slope_v = row_derivative(v, near[v_rows, :].astype(F32), far[v_rows, :].astype(F32), edge, factor)
        along_u = column_derivative(u, left[u_rows, :1], right[u_rows, :1], start, width * peers)
        along_v = column_derivative(v, left[v_rows, :1], right[v_rows, :1], start, width * peers)
        source = lax.rem(where_ref[0] + peers - offset, peers)
        lines = pl.ds(pl.multiple_of(source * frames, frames), frames)
        snap_ref[0, lines, :] = along_u.astype(BF16)
        snap_ref[1, lines, :] = slope_v.astype(BF16)
        snap_ref[2, lines, :] = (0.5 * (slope_u + along_v)).astype(BF16)
    pairs = upper_blocks(total // BLOCK)
    half = len(pairs) // 2
    for i in range(total // BLOCK):
        sums = None
        for c in range(3):
            left = snap_ref[c, span(i), :]
            right = snap_ref[c, i * BLOCK:, :]
            part = lax.dot_general(left, right, (((1,), (1,)), ((), ())), preferred_element_type=F32)
            sums = part if sums is None else sums + part
        for n, (line, col) in enumerate(pairs):
            if line == i:
                both_ref[n // half, n % half] = sums[:, (col - i) * BLOCK:(col - i + 1) * BLOCK]
    core = where_ref[3]
    kept_ref[...] = both_ref[core]
    sent_ref[...] = both_ref[1 - core]


def cross_products(where, parts, total):
    width = parts[0].shape[2]
    count = total // BLOCK
    half = count * (count + 1) // 4
    part = jax.ShapeDtypeStruct((half, BLOCK, BLOCK), F32)
    return pl.pallas_call(
        gram_kernel,
        in_specs=[SMEM] + [VMEM] * len(parts),
        out_specs=[VMEM] * 3,
        out_shape=[jax.ShapeDtypeStruct((3, total, width), BF16), part, part],
        scratch_shapes=[pltpu.VMEM((2, half, BLOCK, BLOCK), F32)],
        compiler_params=PARAMS,
        name="gram_kernel",
    )(where, *parts)


def split(x):
    top = x.astype(BF16).astype(F32)
    rest = x - top
    middle = rest.astype(BF16).astype(F32)
    return top, middle, rest - middle


LEFT = (0, 0, 1, 1, 0, 2)
RIGHT = (0, 1, 0, 1, 2, 0)
TURNED = (((0,), (0,)), ((), ()))
PLAIN = (((1,), (0,)), ((), ()))


def thin_product(left, right):
    lefts, rights = split(left), split(right)
    lefts = jnp.concatenate([lefts[p] for p in LEFT], 0).astype(BF16)
    rights = jnp.concatenate([rights[p] for p in RIGHT], 0).astype(BF16)
    return lax.dot_general(lefts, rights, TURNED, preferred_element_type=F32)


def long_product(left, right, turned):
    lefts = jnp.concatenate([left[p] for p in LEFT], 0 if turned else 1)
    rights = jnp.concatenate([right[p] for p in RIGHT], 0)
    return lax.dot_general(lefts, rights, TURNED if turned else PLAIN, preferred_element_type=F32)


def eliminate_block(rows, fillers, spread_ref):
    tiles = len(rows)
    lane = lax.broadcasted_iota(jnp.int32, (SUB, BLOCK), 1)
    sub = lax.broadcasted_iota(jnp.int32, (SUB, BLOCK), 0)
    upper, inverse = [], []
    rows = list(rows)
    for step in range(tiles):
        for _ in range(-(-len(fillers) // (tiles - step))):
            fillers.pop(0)()
        base = step * SUB
        block = rows[step]
        a = {}
        for j in range(SUB):
            spread_ref[step % 2, j * SUB:(j + 1) * SUB, :] = jnp.broadcast_to(block[:, base + j:base + j + 1], (SUB, BLOCK))
            for i in range(j, SUB):
                a[i, j] = spread_ref[step % 2, pl.ds(j * SUB + i, SUB, stride=0), :]
        inside = (lane >= base) & (lane < base + SUB)
        seeded = jnp.where(inside, (lane - base == sub).astype(F32), block)
        spread_ref[step % 2, SUB * SUB:SUB * (SUB + 1), :] = seeded
        v = [spread_ref[step % 2, pl.ds(SUB * SUB + i, SUB, stride=0), :] for i in range(SUB)]
        unit = {}
        pivot, root = [], []
        for j in range(SUB):
            inv = 1.0 / a[j, j]
            pivot.append(inv)
            root.append(lax.rsqrt(a[j, j]))
            for i in range(j + 1, SUB):
                unit[i, j] = a[i, j] * inv
            for m in range(j + 1, SUB):
                for i in range(m, SUB):
                    a[i, m] = a[i, m] - (a[i, j] * a[m, j]) * inv
            for i in range(j + 1, SUB):
                v[i] = v[i] - unit[i, j] * v[j]
        z = [v[j] * pivot[j] for j in range(SUB)]
        done = jnp.zeros((SUB, BLOCK), F32)
        corner = jnp.zeros((SUB, BLOCK), F32)
        for i in range(SUB):
            line = jnp.zeros((SUB, BLOCK), F32)
            for m in range(i, SUB):
                line = jnp.where(lane == base + m, a[m, i], line)
            done = jnp.where(sub == i, v[i] * root[i], done)
            corner = jnp.where(sub == i, line * root[i], corner)
        upper.append(jnp.where(lane >= base + SUB, done, corner))
        inverse.append(jnp.where(lane < base + SUB, done, 0.0))
        for q in range(step + 1, min(step + 1 + NEAR, tiles)):
            old = rows[q]
            acc = jnp.where(inside, 0.0, old)
            left = [jnp.broadcast_to(old[:, base + j:base + j + 1], (SUB, BLOCK)) for j in range(SUB)]
            for j in range(SUB):
                for m in range(j + 1, SUB):
                    left[m] = left[m] - left[j] * unit[m, j]
                acc = acc - left[j] * z[j]
            rows[q] = acc
        if step + 1 + NEAR < tiles:
            update = thin_product(done, done)
            for q in range(step + 1 + NEAR, tiles):
                rows[q] = jnp.where(inside, 0.0, rows[q]) - update[q * SUB:(q + 1) * SUB, :]
    return upper, inverse


def span(k):
    return slice(k * BLOCK, (k + 1) * BLOCK)


def factor_kernel(where_ref, kept_ref, other_ref, snap_ref, factor_hbm, basis_hbm, gram_ref, carry_ref, part_ref, factor_ref, basis_ref, spread_ref, sems, *, scale):
    n = factor_ref.shape[0]
    blocks = n // BLOCK
    core = where_ref[3]
    gram_ref[core] = kept_ref[...]
    gram_ref[1 - core] = other_ref[...]
    place = {pair: index for index, pair in enumerate(upper_blocks(blocks))}
    half = len(place) // 2

    def gram(i, m):
        return gram_ref.at[place[i, m] // half, place[i, m] % half]

    def carried(i, j):
        return carry_ref.at[i * (i - 1) // 2 + j]

    def parts(k, m):
        return [part_ref[k, p, :, span(m)] for p in range(3)]

    def keep(k, m, value):
        for p, part in enumerate(split(value)):
            part_ref[k, p, :, span(m)] = part.astype(BF16)

    def upper_panel(k, m):
        value = long_product(parts(k, k), split_block(gram(k, m)[...]), False)
        factor_ref[span(k), span(m)] = value * (1.0 / scale)
        keep(k, m, value)

    def split_block(value):
        return [part.astype(BF16) for part in split(value)]

    def update_gram(k, i, m):
        ref = gram(i, m)
        ref[...] = ref[...] - long_product(parts(k, i), parts(k, m), True)

    def update_carried(k, i, j):
        ref = carried(i, j)
        product = long_product(parts(k, i), parts(k, j), True)
        ref[...] = -product if j == k else ref[...] - product

    def lower_panel(k, j):
        keep(k, j, long_product(parts(k, k), split_block(carried(k, j)[...]), False))

    def basis_rows(k, c):
        depth = (k + 1) * BLOCK
        snap = snap_ref[c, :depth, :]
        total = jnp.dot(part_ref[k, 0, :, :depth], snap, preferred_element_type=F32)
        total = total + jnp.dot(part_ref[k, 1, :, :depth], snap, preferred_element_type=F32)
        basis_ref[c, span(k), :] = (total * scale).astype(BF16)

    def copies(k):
        return (
            pltpu.make_async_copy(basis_ref.at[:, span(k), :], basis_hbm.at[:, span(k), :], sems.at[0, k]),
            pltpu.make_async_copy(factor_ref.at[span(k), :], factor_hbm.at[span(k), :], sems.at[1, k]),
        )

    def send(k):
        for copy in copies(k):
            copy.start()

    fillers = []
    for k in range(blocks):
        diagonal = gram(k, k)
        rows = [diagonal[s:s + SUB, :] for s in range(0, BLOCK, SUB)]
        upper, inverse = eliminate_block(rows, fillers, spread_ref)
        keep(k, k, jnp.concatenate(inverse, 0))
        factor_ref[span(k), span(k)] = jnp.concatenate(upper, 0) * (1.0 / scale)
        if k:
            factor_ref[span(k), :k * BLOCK] = jnp.zeros((BLOCK, k * BLOCK), F32)
        later = range(k + 1, blocks)
        if later:
            upper_panel(k, k + 1)
            update_gram(k, k + 1, k + 1)
        fillers = [functools.partial(upper_panel, k, m) for m in later[1:]]
        fillers += [functools.partial(lower_panel, k, j) for j in range(k)]
        fillers += [functools.partial(update_gram, k, i, m) for i in later for m in range(i, blocks) if (i, m) != (k + 1, k + 1)]
        fillers += [functools.partial(update_carried, k, i, j) for i in later for j in range(k + 1)]
        fillers += [functools.partial(basis_rows, k, c) for c in range(snap_ref.shape[0])]
        fillers.append(functools.partial(send, k))
    for filler in fillers:
        filler()
    for k in range(blocks):
        for copy in copies(k):
            copy.wait()


def factorize(where, kept, other, snap, scale):
    n = snap.shape[1]
    blocks = n // BLOCK
    return pl.pallas_call(
        functools.partial(factor_kernel, scale=scale),
        in_specs=[SMEM, VMEM, VMEM, VMEM],
        out_specs=[pl.BlockSpec(memory_space=pl.ANY)] * 2,
        out_shape=[jax.ShapeDtypeStruct((n, n), F32), jax.ShapeDtypeStruct(snap.shape, BF16)],
        scratch_shapes=[
            pltpu.VMEM((2,) + kept.shape, F32),
            pltpu.VMEM((blocks * (blocks - 1) // 2, BLOCK, BLOCK), F32),
            pltpu.VMEM((blocks, 3, BLOCK, n), BF16),
            pltpu.VMEM((n, n), F32),
            pltpu.VMEM(snap.shape, BF16),
            pltpu.VMEM((2, SUB * (SUB + 2), BLOCK), F32),
            pltpu.SemaphoreType.DMA((2, blocks)),
        ],
        compiler_params=PARAMS,
        name="factor_kernel",
    )(where, kept, other, snap)


def sum_devices(kept, sent):
    swap = [(0, 1), (1, 0)]
    shape = kept.shape
    kept = (kept + lax.ppermute(sent, "core", swap)).reshape(-1, shape[-1])
    plane = lax.axis_size(("x", "y"))
    part, width = kept.shape[0] // plane, kept.shape[1]
    piece = lax.all_to_all(kept.reshape(plane, part, width), ("x", "y"), 0, 0, tiled=True).sum(0)
    copies = jnp.broadcast_to(piece[None], (lax.axis_size("z"), part, width))
    piece = lax.all_to_all(copies, "z", 0, 0, tiled=True).sum(0)
    copies = jnp.broadcast_to(piece[None], (plane, part, width))
    kept = lax.all_to_all(copies, ("x", "y"), 0, 0, tiled=True).reshape(shape)
    return kept, lax.ppermute(kept, "core", swap)


def local(displacement):
    frames, _, _, width = displacement.shape
    peers = lax.axis_size("z")
    total_rows = lax.axis_size(TILE)
    total_frames = frames * peers
    scale = math.sqrt(3 * total_rows * width)
    where = jnp.stack([lax.axis_index("z"), lax.axis_index(TILE), jnp.int32(total_rows), lax.axis_index("core")]).astype(jnp.int32)
    planes = displacement.reshape(frames, 2, width).transpose(1, 0, 2)
    first, second = exchange(where, planes, peers)
    chip = [(i, i ^ 1) for i in range(total_rows)]
    between = [(i, ((i + 1) ^ 1) - 1) for i in range(1, total_rows - 1)]
    inner = [lax.ppermute(part, TILE, chip) for part in (first, second)]
    outer = [lax.ppermute(part, TILE, between) for part in (first, second)]
    snap, kept, sent = cross_products(where, [first, second] + inner + outer, total_frames)
    kept, other = sum_devices(kept, sent)
    factor, basis = factorize(where, kept, other, snap, scale)
    return basis.transpose(1, 0, 2)[:, :, None, :], factor


def solution(mesh):
    frames, tiles = mesh.devices.shape
    side = math.isqrt(tiles // 2)
    split = Mesh(mesh.devices.reshape(frames, side, side, 2), ("z",) + TILE)
    return jax.shard_map(
        local,
        mesh=split,
        in_specs=(P("z", None, TILE, None),),
        out_specs=(P(None, None, TILE, "z"), P()),
        check_vma=False,
    )
```
